32 devices in a mesh: ens: 2 (over y), lat: 4 (over x, core), lon: 4 (over z).
Axes of the slice: x: 2, y: 2, z: 4, core: 2. Of those that a mesh axis runs over, the one named last changes fastest.
Arguments:
- state_now: float32 [6, 1152, 2304], P('ens', 'lat', 'lon'), parts along dimension 0, may hold values from -2 to 2, as said below
- state_old: float32 [6, 1152, 2304], P('ens', 'lat', 'lon'), parts along dimension 0, may hold values from -6 to 6
- polar_cutoff: int32 [576], replicated, may hold values from 1 to 1152, as said below
Outputs:
- state_new: float32 [6, 1152, 2304], P('ens', 'lat', 'lon'), parts along dimension 0
The draws below stay inside these ranges and needn't reach their ends.
There are 2 independent parts, one for each index of `ens`. The reference program is written for one: setup_inputs(seed, part) draws one part's arguments, and reference() takes and returns one part's arrays. A program takes and returns all parts, laid end to end along the dimension named above; an argument that names none is the same for every part. Nothing has to cross between parts.
Inputs may be any that keep to these rules, and one draw needn't show every extreme that they name: `polar_cutoff`: every entry is at least 1 and at most 1152; the two rows next to 45 degrees keep all wavenumbers up to 1152. `state_now`: component 0 (depth) lies between 0.25 and 1.75.
All inputs are finite; a program needn't handle non-finite values.
Results may differ from the reference program's by a relative error of at most 0.00005.
Values sent between devices are 32-bit elements; how exact they have to be, the bound alone decides.
A program may use at most 64 MiB of HBM per device.

```python
import math
import jax
import jax.numpy as jnp

NLON = 2304
NLAT = 1152


def draw_state_now(key, part):
    first_key, second_key = jax.random.split(jax.random.fold_in(key, 11))
    depth = 1.0 + 0.25 * jnp.clip(jax.random.normal(first_key, (NLAT, NLON), jnp.float32), -3.0, 3.0)
    wind = 0.5 * jnp.clip(jax.random.normal(second_key, (2, NLAT, NLON), jnp.float32), -4.0, 4.0)
    return jnp.concatenate([depth[None], wind], axis=0).astype(jnp.float32)


def draw_polar_cutoff(key, part):
    quarter = NLAT // 4
    steps_in = jnp.arange(quarter, dtype=jnp.int32)
    distance = jnp.concatenate([steps_in, quarter - 1 - steps_in])
    base_cut = jnp.maximum((distance + 1) * (NLON // 2) // quarter, 2)
    jitter = jax.random.randint(jax.random.fold_in(key, 23), (2 * quarter,), 0, base_cut // 2 + 1, dtype=jnp.int32)
    jitter = jnp.where(distance == quarter - 1, 0, jitter)
    return (base_cut - jitter).astype(jnp.int32)


def block_levels(own_key, extent, pieces, least, largest):
    def one(position, parts):
        draws = jax.random.uniform(jax.random.fold_in(jax.random.fold_in(own_key, 6), position), (parts,), jnp.float32, least / len(pieces), largest / len(pieces))
        return jnp.repeat(jnp.exp(draws), extent[position] // parts).reshape((-1,) + (1,) * (len(extent) - position - 1))

    loudness = one(*pieces[0])
    for cut in pieces[1:]:
        loudness = loudness * one(*cut)
    return loudness


def bell_draw(stream_key, extent, spread, bound, cuts=(), held_as=jnp.bfloat16):
    values = jax.random.normal(stream_key, extent, jnp.float32) * spread
    if len(cuts) > 0:
        values = block_levels(stream_key, extent, cuts, -0.22, 0.18) * values
    return jnp.clip(values, min=-bound, max=bound).astype(held_as)


def setup_inputs(seed: int = 0, part: int = 0) -> dict:
    streams_of = jax.random.split(jax.random.key(seed), 4)
    part_keys = jax.random.split(jax.random.fold_in(streams_of[3], part), 4)
    return {
        "state_now": draw_state_now(jax.random.fold_in(jax.random.fold_in(streams_of[3], part), 71), part),
        "state_old": bell_draw(part_keys[1], (3, NLAT, NLON), 1.0, 6.0, ((1, 4), (2, 4)), jnp.float32),
        "polar_cutoff": draw_polar_cutoff(jax.random.fold_in(streams_of[3], 71), part),
    }


step_scale = 0.2
coriolis = 2.0
gravity = 1.0


def latitude_terms(row_index, lat_total):
    distance = jnp.minimum(row_index + 0.5, lat_total - row_index - 0.5)
    cosine_lat = jnp.sin(math.pi * distance / lat_total)
    sine_lat = -jnp.cos(math.pi * (row_index + 0.5) / lat_total)
    return cosine_lat, sine_lat


def tendencies(lat_padded, lon_padded, cos_ext, sine_lat, lat_total, lon_total):
    cosine_lat = cos_ext[1:-1]
    zonal_scale = (lon_total / (4.0 * lat_total) / cosine_lat)[:, None]
    metric = (math.pi / lat_total) * sine_lat / cosine_lat
    depth_lon, east_lon, north_lon = lon_padded[0], lon_padded[1], lon_padded[2]
    depth_lat, east_lat, north_lat = lat_padded[0], lat_padded[1], lat_padded[2]
    depth = depth_lon[:, 1:-1]
    east = east_lon[:, 1:-1]
    north = north_lon[:, 1:-1]

    def zonal_change(field):
        return zonal_scale * (field[:, 2:] - field[:, :-2])

    def northward_change(field):
        return 0.5 * (field[2:] - field[:-2])

    mass_flux = depth_lat * north_lat * cos_ext[:, None]
    tend_depth = -zonal_change(depth_lon * east_lon) - northward_change(mass_flux) / cosine_lat[:, None]
    turning = coriolis * sine_lat[:, None] + metric[:, None] * east
    tend_east = -east * zonal_change(east_lon) - north * northward_change(east_lat) + turning * north - gravity * zonal_change(depth_lon)
    tend_north = -east * zonal_change(north_lon) - north * northward_change(north_lat) - turning * east - gravity * northward_change(depth_lat)
    return jnp.stack([tend_depth, tend_east, tend_north])


def reference(state_now, state_old, polar_cutoff):
    row_index = jnp.arange(-1, NLAT + 1, dtype=jnp.int32).astype(jnp.float32)
    cos_ext, sin_ext = latitude_terms(row_index, NLAT)
    lat_padded = jnp.pad(state_now, ((0, 0), (1, 1), (0, 0)))
    lon_padded = jnp.concatenate([state_now[:, :, -1:], state_now, state_now[:, :, :1]], axis=2)
    forcing = tendencies(lat_padded, lon_padded, cos_ext, sin_ext[1:-1], NLAT, NLON)
    quarter = NLAT // 4
    polar_rows = jnp.concatenate([forcing[:, :quarter], forcing[:, NLAT - quarter:]], axis=1)
    spectrum = jnp.fft.rfft(polar_rows, axis=2)
    wavenumber = jnp.arange(NLON // 2 + 1, dtype=jnp.int32)
    keep_mask = wavenumber[None, None, :] <= polar_cutoff[None, :, None]
    smooth = jnp.fft.irfft(jnp.where(keep_mask, spectrum, 0.0), n=NLON, axis=2).astype(forcing.dtype)
    filtered = forcing.at[:, :quarter].set(smooth[:, :quarter]).at[:, NLAT - quarter:].set(smooth[:, quarter:])
    return state_old + step_scale * filtered
```

```python
import functools
import math

import jax
import jax.numpy as jnp
import numpy as np
from jax import lax
from jax.experimental import pallas as pl
from jax.experimental.pallas import tpu as pltpu
from jax.sharding import PartitionSpec as P

LANES = 128
SUB = 8
MESH = pl.DeviceIdType.MESH
step_scale = 0.2
coriolis = 2.0
gravity = 1.0
highest = lax.Precision.HIGHEST


def padded(value, sides, width, wrap):
    for axis, dim in sides:
        devices, length = (lax.axis_size(axis), value.shape[dim])
        up = [(i, (i + 1) % devices) for i in range(devices if wrap else devices - 1)]
        down = [(j, i) for i, j in up]
        last = lax.slice_in_dim(value, length - width, length, axis=dim)
        leading = lax.slice_in_dim(value, 0, width, axis=dim)
        before = lax.ppermute(last, axis, up)
        after = lax.ppermute(leading, axis, down)
        value = jnp.concatenate([before, value, after], axis=dim)
    return value


def latitude_terms(row_index, lat_total):
    distance = jnp.minimum(row_index + 0.5, lat_total - row_index - 0.5)
    cosine_lat = jnp.sin(math.pi * distance / lat_total)
    sine_lat = -jnp.cos(math.pi * (row_index + 0.5) / lat_total)
    return (cosine_lat, sine_lat)


def tendencies(lat_padded, lon_padded, cos_ext, sine_lat, lat_total, lon_total):
    cosine_lat = cos_ext[1:-1]
    zonal_scale = (lon_total / (4.0 * lat_total) / cosine_lat)[:, None]
    metric = math.pi / lat_total * sine_lat / cosine_lat
    depth_lon, east_lon, north_lon = (lon_padded[0], lon_padded[1], lon_padded[2])
    depth_lat, east_lat, north_lat = (lat_padded[0], lat_padded[1], lat_padded[2])
    east = east_lon[:, 1:-1]
    north = north_lon[:, 1:-1]

    def zonal_change(field):
        return zonal_scale * (field[:, 2:] - field[:, :-2])

    def northward_change(field):
        return 0.5 * (field[2:] - field[:-2])

    mass_flux = depth_lat * north_lat * cos_ext[:, None]
    tend_depth = (
        -zonal_change(depth_lon * east_lon) - northward_change(mass_flux) / cosine_lat[:, None]
    )
    turning = coriolis * sine_lat[:, None] + metric[:, None] * east
    tend_east = (
        -east * zonal_change(east_lon)
        - north * northward_change(east_lat)
        + turning * north
        - gravity * zonal_change(depth_lon)
    )
    tend_north = (
        -east * zonal_change(north_lon)
        - north * northward_change(north_lat)
        - turning * east
        - gravity * northward_change(depth_lat)
    )
    return jnp.stack([tend_depth, tend_east, tend_north])


def angle_table(first_count, second_count, period):
    first_idx = jnp.arange(first_count, dtype=jnp.int32)
    second_idx = jnp.arange(second_count, dtype=jnp.int32)
    turns = first_idx[:, None] * second_idx[None, :] % period
    phase = turns.astype(jnp.float32) * (2.0 * math.pi / period)
    return (jnp.cos(phase), jnp.sin(phase))


def low_pass(signal, cutoff):
    count, length = signal.shape
    first = 1
    probe = 1
    while probe * probe <= length:
        if length % probe == 0:
            first = probe
        probe = probe + 1
    second = length // first
    cos_first, sin_first = angle_table(first, first, first)
    cos_second, sin_second = angle_table(second, second, second)
    cos_twist, sin_twist = angle_table(first, second, length)
    grid = signal.reshape(count, first, second)
    part_re = jnp.einsum("cpq,pk->ckq", grid, cos_first, precision=highest)
    part_im = -jnp.einsum("cpq,pk->ckq", grid, sin_first, precision=highest)
    twist_re = part_re * cos_twist + part_im * sin_twist
    twist_im = part_im * cos_twist - part_re * sin_twist
    spec_re = jnp.einsum("ckq,qm->ckm", twist_re, cos_second, precision=highest) + jnp.einsum(
        "ckq,qm->ckm", twist_im, sin_second, precision=highest
    )
    spec_im = jnp.einsum("ckq,qm->ckm", twist_im, cos_second, precision=highest) - jnp.einsum(
        "ckq,qm->ckm", twist_re, sin_second, precision=highest
    )
    wave = (
        jnp.arange(first, dtype=jnp.int32)[:, None]
        + first * jnp.arange(second, dtype=jnp.int32)[None, :]
    )
    limit = cutoff[:, None, None]
    keep = ((wave[None] <= limit) | (wave[None] >= length - limit)).astype(jnp.float32) * (
        1.0 / length
    )
    spec_re = spec_re * keep
    spec_im = spec_im * keep
    back_re = jnp.einsum("ckm,mq->ckq", spec_re, cos_second, precision=highest) - jnp.einsum(
        "ckm,mq->ckq", spec_im, sin_second, precision=highest
    )
    back_im = jnp.einsum("ckm,mq->ckq", spec_im, cos_second, precision=highest) + jnp.einsum(
        "ckm,mq->ckq", spec_re, sin_second, precision=highest
    )
    turn_re = back_re * cos_twist - back_im * sin_twist
    turn_im = back_im * cos_twist + back_re * sin_twist
    result = jnp.einsum("ckq,kp->cpq", turn_re, cos_first, precision=highest) - jnp.einsum(
        "ckq,kp->cpq", turn_im, sin_first, precision=highest
    )
    return result.reshape(count, length)


def per_device(state_now, state_old, polar_cutoff):
    lat_rows = state_now.shape[1]
    lon_cols = state_now.shape[2]
    lat_count = lax.axis_size("lat")
    lon_count = lax.axis_size("lon")
    lat_total = lat_rows * lat_count
    lon_total = lon_cols * lon_count
    lat_place = lax.axis_index("lat")
    lat_padded = padded(state_now, (("lat", 1),), 1, False)
    lon_padded = padded(state_now, (("lon", 2),), 1, True)
    row_index = (lat_place * lat_rows + jnp.arange(-1, lat_rows + 1, dtype=jnp.int32)).astype(
        jnp.float32
    )
    cos_ext, sin_ext = latitude_terms(row_index, lat_total)
    forcing = tendencies(lat_padded, lon_padded, cos_ext, sin_ext[1:-1], lat_total, lon_total)
    groups = lat_count * lon_count
    share = lat_rows // groups
    member = lax.axis_index(("lat", "lon"))
    south_cut = lax.dynamic_slice_in_dim(polar_cutoff, member * share, share)
    north_cut = lax.dynamic_slice_in_dim(polar_cutoff, lat_rows + member * share, share)
    band_cut = jnp.concatenate([south_cut, north_cut])
    block = lax.all_to_all(forcing, ("lat", "lon"), split_axis=1, concat_axis=2, tiled=True)
    items = block.shape[0]
    wide = block.shape[2]
    south_rows = block[:, :, :lon_total]
    north_rows = block[:, :, wide - lon_total :]
    polar_rows = jnp.concatenate([south_rows, north_rows], axis=1)
    smooth = low_pass(polar_rows.reshape(items * 2 * share, lon_total), jnp.tile(band_cut, items))
    smooth = smooth.reshape(items, 2 * share, lon_total)
    rebuilt = jnp.concatenate(
        [smooth[:, :share], block[:, :, lon_total : wide - lon_total], smooth[:, share:]], axis=2
    )
    filtered = lax.all_to_all(rebuilt, ("lat", "lon"), split_axis=2, concat_axis=1, tiled=True)
    return state_old + step_scale * filtered


def spectral_tables(total):
    tiles = total // LANES
    half = tiles // 2
    q = np.arange(LANES)[:, None]
    m = np.arange(LANES)[None, :]
    forward = np.zeros((half, 2 * LANES, 2 * LANES))
    inverse = np.zeros((half, 2 * LANES, 2 * LANES))
    wave = np.zeros((half, 2 * LANES), np.int64)

    def angle(k):
        return 2.0 * np.pi * ((q * k) % total) / total

    mid = LANES // 2
    re_m = np.arange(mid + 1)[None, :]
    im_m = np.arange(1, mid)[None, :]
    weight = np.where((re_m == 0) | (re_m == mid), 1.0, 2.0) / total
    k_re, k_im = tiles * re_m, tiles * im_m
    forward[0, :LANES, : mid + 1] = np.cos(angle(k_re))
    forward[0, :LANES, mid + 1 : LANES] = -np.sin(angle(k_im))
    inverse[0, : mid + 1, :LANES] = (np.cos(angle(k_re)) * weight).T
    inverse[0, mid + 1 : LANES, :LANES] = (-np.sin(angle(k_im)) * 2.0 / total).T
    k_odd = half + tiles * np.arange(mid)[None, :]
    odd = np.concatenate([np.cos(angle(k_odd)), -np.sin(angle(k_odd))], axis=1)
    forward[0, LANES:, LANES:] = odd
    inverse[0, LANES:, LANES:] = odd.T * 2.0 / total
    wave[0] = np.concatenate([k_re[0], k_im[0], k_odd[0], k_odd[0]])
    for r in range(1, half):
        k = r + tiles * m
        c, s = np.cos(angle(k)), np.sin(angle(k))
        forward[r] = np.block([[c, -s], [s, c]])
        inverse[r] = forward[r].T * 2.0 / total
        wave[r] = np.concatenate([k[0], k[0]])
    wave = np.minimum(wave, total - wave)

    def split(a):
        a = a.astype(np.float32)
        hi = a.astype(jnp.bfloat16)
        lo = (a - hi.astype(np.float32)).astype(jnp.bfloat16)
        return np.stack([hi, lo])

    wave = np.broadcast_to(wave[:, None, :], (half, SUB, 2 * LANES)).astype(np.int32)
    return split(forward), split(inverse), np.ascontiguousarray(wave)


def geometry_table(lat_total, lon_total):
    j = np.arange(lat_total, dtype=np.float64)

    def cosine(row):
        return np.sin(np.pi * np.minimum(row + 0.5, lat_total - row - 0.5) / lat_total)

    c = cosine(j)
    s = -np.cos(np.pi * (j + 0.5) / lat_total)
    table = np.zeros((lat_total, LANES))
    table[:, 0] = lon_total / (4.0 * lat_total * c)
    table[:, 1] = 0.5 * cosine(j + 1) / c
    table[:, 2] = 0.5 * cosine(j - 1) / c
    table[:, 3] = coriolis * s
    table[:, 4] = np.pi / lat_total * s / c
    return table.astype(np.float32)


def forward_radix(tile, tiles):
    half = tiles // 2
    x = [tile(p) for p in range(tiles)]
    even = [None] * (half + 1)
    odd = [None] * (half + 1)
    even[0], even[half] = x[0], x[half]
    for p in range(1, half):
        even[p] = x[p] + x[tiles - p]
        odd[p] = x[p] - x[tiles - p]
    re, im = [None] * (half + 1), [None] * (half + 1)
    for r in range(half // 2 + 1):
        e = parity_sum([(even[p], math.cos(2 * math.pi * p * r / tiles)) for p in range(0, half + 1, 2)])
        o = parity_sum([(even[p], math.cos(2 * math.pi * p * r / tiles)) for p in range(1, half + 1, 2)])
        re[r] = e + o
        re[half - r] = e - o
        if 0 < r:
            es = parity_sum([(odd[p], math.sin(2 * math.pi * p * r / tiles)) for p in range(2, half, 2)])
            os = parity_sum([(odd[p], math.sin(2 * math.pi * p * r / tiles)) for p in range(1, half, 2)])
            im[r] = -(es + os)
            im[half - r] = es - os
    return re, im


def parity_sum(terms):
    total = None
    for value, factor in terms:
        if abs(factor - 1.0) < 1e-12:
            term = value
        elif abs(factor + 1.0) < 1e-12:
            term = -value
        elif abs(factor) < 1e-12:
            continue
        else:
            term = value * np.float32(factor)
        total = term if total is None else total + term
    return total if total is not None else jnp.zeros_like(terms[0][0])


def inverse_radix(re, im, tiles):
    half = tiles // 2
    x = [None] * tiles
    for p in range(half // 2 + 1):
        ce = parity_sum([(re[r], math.cos(2 * math.pi * p * r / tiles)) for r in range(0, half + 1, 2)])
        co = parity_sum([(re[r], math.cos(2 * math.pi * p * r / tiles)) for r in range(1, half + 1, 2)])
        if p == 0:
            x[0] = ce + co
            x[half] = ce - co
            continue
        se = parity_sum([(im[r], math.sin(2 * math.pi * p * r / tiles)) for r in range(2, half, 2)])
        so = parity_sum([(im[r], math.sin(2 * math.pi * p * r / tiles)) for r in range(1, half, 2)])
        c, s = ce + co, se + so
        x[p] = c - s
        x[tiles - p] = c + s
        c, s = ce - co, so - se
        x[half - p] = c - s
        x[half + p] = c + s
    return x


def split_dot(value, table, r):
    hi = value.astype(jnp.bfloat16)
    lo = (value - hi.astype(jnp.float32)).astype(jnp.bfloat16)
    big, small = table[0, r], table[1, r]
    out = jnp.dot(hi, big, preferred_element_type=jnp.float32)
    out = out + jnp.dot(lo, big, preferred_element_type=jnp.float32)
    return out + jnp.dot(hi, small, preferred_element_type=jnp.float32)


def step_kernel(
    lat_count, lon_count, chunk,
    x_hbm, geo_hbm, cut_ref, wave_ref, fwd_hbm, inv_hbm, out_ref,
    xp, geo, tend, recv, ret, full, spec, fwd, inv, col_send, col_recv,
    load_sem, table_sem, row_send_sem, row_recv_sem, col_send_sem, col_recv_sem,
    go_send, go_recv, back_send, back_recv, own_sem,
):
    rows, cols = out_ref.shape[1], out_ref.shape[2]
    share = rows // lon_count
    chunks = share // chunk
    groups = rows // SUB
    tiles = lon_count * cols // LANES
    half = tiles // 2
    lat = lax.axis_index("lat")
    lon = lax.axis_index("lon")
    west = lax.rem(lon + lon_count - 1, lon_count)
    east = lax.rem(lon + 1, lon_count)
    polar = jnp.logical_or(lat == 0, lat == lat_count - 1)
    has_south = lat > 0
    has_north = lat < lat_count - 1

    load = pltpu.make_async_copy(x_hbm, xp.at[:, pl.ds(SUB, rows), :], load_sem)
    load.start()
    geo_load = pltpu.make_async_copy(
        geo_hbm.at[pl.ds(pl.multiple_of(lat * rows, SUB), rows), :], geo, table_sem.at[0]
    )
    geo_load.start()
    fwd_load = pltpu.make_async_copy(fwd_hbm, fwd, table_sem.at[1])
    inv_load = pltpu.make_async_copy(inv_hbm, inv, table_sem.at[2])
    fwd_load.start()
    inv_load.start()

    barrier = pltpu.get_barrier_semaphore()
    for k in range(1, lon_count):
        pl.semaphore_signal(
            barrier, inc=1, device_id={"lon": lax.rem(lon + k, lon_count)}, device_id_type=MESH
        )

    @pl.when(has_south)
    def _():
        pl.semaphore_signal(barrier, inc=1, device_id={"lat": lat - 1}, device_id_type=MESH)

    @pl.when(has_north)
    def _():
        pl.semaphore_signal(barrier, inc=1, device_id={"lat": lat + 1}, device_id_type=MESH)

    pl.semaphore_wait(
        barrier, lon_count - 1 + has_south.astype(jnp.int32) + has_north.astype(jnp.int32)
    )

    def to_south():
        return pltpu.make_async_remote_copy(
            src_ref=x_hbm.at[:, pl.ds(0, SUB), :], dst_ref=xp.at[:, pl.ds(rows + SUB, SUB), :],
            send_sem=row_send_sem.at[0], recv_sem=row_recv_sem.at[0],
            device_id={"lat": lat - 1}, device_id_type=MESH,
        )

    def to_north():
        return pltpu.make_async_remote_copy(
            src_ref=x_hbm.at[:, pl.ds(rows - SUB, SUB), :], dst_ref=xp.at[:, pl.ds(0, SUB), :],
            send_sem=row_send_sem.at[1], recv_sem=row_recv_sem.at[1],
            device_id={"lat": lat + 1}, device_id_type=MESH,
        )

    @pl.when(has_south)
    def _():
        to_south().start()

    @pl.when(has_north)
    def _():
        to_north().start()

    zero_rows = jnp.zeros((3, SUB, cols), jnp.float32)

    @pl.when(jnp.logical_not(has_south))
    def _():
        xp[:, 0:SUB, :] = zero_rows

    @pl.when(jnp.logical_not(has_north))
    def _():
        xp[:, rows + SUB : rows + 2 * SUB, :] = zero_rows

    load.wait()
    lane = lax.broadcasted_iota(jnp.int32, (SUB, LANES), 1)

    packed = [jnp.zeros((SUB, LANES), jnp.float32) for _ in range(6)]
    for g in range(groups):
        here = lane == g
        for c in range(3):
            block = slice(SUB + g * SUB, 2 * SUB + g * SUB)
            packed[2 * c] = jnp.where(here, xp[c, block, 0:1], packed[2 * c])
            packed[2 * c + 1] = jnp.where(here, xp[c, block, cols - 1 : cols], packed[2 * c + 1])
    for c in range(3):
        col_send[0, c] = packed[2 * c]
        col_send[1, c] = packed[2 * c + 1]

    def column_copy(side, target):
        return pltpu.make_async_remote_copy(
            src_ref=col_send.at[side], dst_ref=col_recv.at[side],
            send_sem=col_send_sem.at[side], recv_sem=col_recv_sem.at[side],
            device_id={"lon": target}, device_id_type=MESH,
        )

    first_out = column_copy(0, west)
    last_out = column_copy(1, east)
    first_out.start()
    last_out.start()
    geo_load.wait()
    first_out.wait()
    last_out.wait()

    @pl.when(has_south)
    def _():
        to_south().wait_send()
        to_north().wait_recv()

    @pl.when(has_north)
    def _():
        to_north().wait_send()
        to_south().wait_recv()

    sub_idx = lax.broadcasted_iota(jnp.int32, (SUB, cols), 0)

    def tendency_group(g):
        start = pl.multiple_of(g * SUB, SUB)
        terms = geo[pl.ds(start, SUB), :]
        zonal, up, down, turn, metric = [terms[:, i : i + 1] for i in range(5)]
        cur, north, south, diff, east_of, west_of = [], [], [], [], [], []
        for c in range(3):
            before = xp[c, pl.ds(start, SUB), :]
            here = xp[c, pl.ds(pl.multiple_of(start + SUB, SUB), SUB), :]
            after = xp[c, pl.ds(pl.multiple_of(start + 2 * SUB, SUB), SUB), :]
            north.append(pltpu.roll(jnp.where(sub_idx == 0, after, here), SUB - 1, 0))
            south.append(pltpu.roll(jnp.where(sub_idx == SUB - 1, before, here), 1, 0))
            on = lane == g
            right = jnp.sum(jnp.where(on, col_recv[0, c], 0.0), axis=1, keepdims=True)
            left = jnp.sum(jnp.where(on, col_recv[1, c], 0.0), axis=1, keepdims=True)
            east_of.append(jnp.concatenate([here[:, 1:], right], axis=1))
            west_of.append(jnp.concatenate([left, here[:, :-1]], axis=1))
            cur.append(here)
        h, u, v = cur
        t_h = -zonal * (east_of[0] * east_of[1] - west_of[0] * west_of[1]) - (
            up * (north[0] * north[2]) - down * (south[0] * south[2])
        )
        turning = turn + metric * u
        zu = zonal * u
        hv = 0.5 * v
        t_u = (
            turning * v - zu * (east_of[1] - west_of[1]) - hv * (north[1] - south[1])
            - zonal * (east_of[0] - west_of[0])
        )
        t_v = (
            -turning * u - zu * (east_of[2] - west_of[2]) - hv * (north[2] - south[2])
            - 0.5 * (north[0] - south[0])
        )
        tend[0, pl.ds(start, SUB), :] = t_h
        tend[1, pl.ds(start, SUB), :] = t_u
        tend[2, pl.ds(start, SUB), :] = t_v

    def aligned(i):
        return pl.multiple_of(i, SUB)

    def go_copy(part, target, source):
        return pltpu.make_async_remote_copy(
            src_ref=tend.at[:, pl.ds(aligned(target * share + part * chunk), chunk), :],
            dst_ref=recv.at[source, :, pl.ds(aligned(part * chunk), chunk), :],
            send_sem=go_send.at[target, part], recv_sem=go_recv.at[source, part],
            device_id={"lon": target}, device_id_type=MESH,
        )

    def back_copy(part, target, source):
        return pltpu.make_async_remote_copy(
            src_ref=ret.at[target, :, pl.ds(aligned(part * chunk), chunk), :],
            dst_ref=out_ref.at[:, pl.ds(aligned(source * share + part * chunk), chunk), :],
            send_sem=back_send.at[target, part], recv_sem=back_recv.at[source, part],
            device_id={"lon": target}, device_id_type=MESH,
        )

    def own_go(part):
        return pltpu.make_async_copy(
            tend.at[:, pl.ds(aligned(lon * share + part * chunk), chunk), :],
            recv.at[lon, :, pl.ds(aligned(part * chunk), chunk), :],
            own_sem.at[0, part],
        )

    def own_back(part):
        return pltpu.make_async_copy(
            ret.at[lon, :, pl.ds(aligned(part * chunk), chunk), :],
            out_ref.at[:, pl.ds(aligned(lon * share + part * chunk), chunk), :],
            own_sem.at[1, part],
        )

    @pl.loop(0, chunks)
    def _(part):
        @pl.loop(1, lon_count + 1)
        def _(k):
            target = lax.rem(lon + k, lon_count)
            first = (target * share + part * chunk) // SUB

            @pl.loop(0, chunk // SUB)
            def _(i):
                tendency_group(first + i)

            @pl.when(jnp.logical_and(polar, k < lon_count))
            def _():
                go_copy(part, target, lon).start()

        @pl.when(polar)
        def _():
            own_go(part).start()

    fwd_load.wait()
    inv_load.wait()

    @pl.when(jnp.logical_not(polar))
    def _():
        keep = pltpu.make_async_copy(tend, out_ref, load_sem)
        keep.start()
        keep.wait()

    @pl.when(polar)
    def _():
        @pl.loop(0, chunks)
        def _(part):
            own_go(part).wait()
            for k in range(1, lon_count):
                source = lax.rem(lon + k, lon_count)
                go_copy(part, lon, source).wait_recv()
            at = pl.ds(aligned(part * chunk), chunk)
            for c in range(3):
                for d in range(lon_count):
                    full[c * chunk : (c + 1) * chunk, d * cols : (d + 1) * cols] = recv[d, c, at, :]

            @pl.loop(0, 3 * chunk // SUB)
            def _(g):
                block = pl.ds(aligned(g * SUB), SUB)
                re, im = forward_radix(lambda p: full[block, p * LANES : (p + 1) * LANES], tiles)
                spec[0, block, :LANES] = re[0]
                spec[0, block, LANES:] = re[half]
                for r in range(1, half):
                    spec[r, block, :LANES] = re[r]
                    spec[r, block, LANES:] = im[r]

            limit = cut_ref[at, :]
            limit = jnp.concatenate([limit, limit], axis=1)
            limit = jnp.concatenate([limit, limit, limit], axis=0)

            @pl.loop(0, half)
            def _(r):
                z = split_dot(spec[r], fwd, r)
                z = jnp.where(wave_ref[r, 0:1, :] <= limit, z, 0.0)
                spec[r] = split_dot(z, inv, r)

            @pl.loop(0, 3 * chunk // SUB)
            def _(g):
                block = pl.ds(aligned(g * SUB), SUB)
                re = [spec[r, block, :LANES] for r in range(half)] + [spec[0, block, LANES:]]
                im = [None] + [spec[r, block, LANES:] for r in range(1, half)]
                x = inverse_radix(re, im, tiles)
                for p in range(tiles):
                    full[block, p * LANES : (p + 1) * LANES] = x[p]

            for c in range(3):
                for d in range(lon_count):
                    ret[d, c, at, :] = full[c * chunk : (c + 1) * chunk, d * cols : (d + 1) * cols]
            own_back(part).start()
            for k in range(1, lon_count):
                back_copy(part, lax.rem(lon + k, lon_count), lon).start()

        @pl.loop(0, chunks)
        def _(part):
            own_back(part).wait()
            for k in range(1, lon_count):
                other = lax.rem(lon + k, lon_count)
                go_copy(part, other, lon).wait_send()
                back_copy(part, other, lon).wait_send()
                back_copy(part, lon, other).wait_recv()


def fused_step(mesh_shape, tables, state_now, state_old, polar_cutoff):
    lat_count, lon_count = mesh_shape
    comps, rows, cols = state_now.shape
    share = rows // lon_count
    total = lon_count * cols
    half = total // LANES // 2
    chunk = chunk_rows(share)
    chunks = share // chunk
    geo, fwd, inv, wave = tables
    lat = lax.axis_index("lat")
    lon = lax.axis_index("lon")
    start = jnp.where(lat == 0, 0, rows) + lon * share
    cut = lax.dynamic_slice_in_dim(polar_cutoff, start, share)
    cut = jnp.broadcast_to(cut[:, None], (share, LANES))
    any_spec = pl.BlockSpec(memory_space=pl.ANY)
    vmem_spec = pl.BlockSpec(memory_space=pltpu.VMEM)
    dma = pltpu.SemaphoreType.DMA
    filtered = pl.pallas_call(
        functools.partial(step_kernel, lat_count, lon_count, chunk),
        out_shape=jax.ShapeDtypeStruct(state_now.shape, jnp.float32),
        in_specs=[any_spec, any_spec, vmem_spec, vmem_spec, any_spec, any_spec],
        out_specs=vmem_spec,
        scratch_shapes=[
            pltpu.VMEM((comps, rows + 2 * SUB, cols), jnp.float32),
            pltpu.VMEM((rows, LANES), jnp.float32),
            pltpu.VMEM((comps, rows, cols), jnp.float32),
            pltpu.VMEM((lon_count, comps, share, cols), jnp.float32),
            pltpu.VMEM((lon_count, comps, share, cols), jnp.float32),
            pltpu.VMEM((comps * chunk, total), jnp.float32),
            pltpu.VMEM((half, comps * chunk, 2 * LANES), jnp.float32),
            pltpu.VMEM((2, half, 2 * LANES, 2 * LANES), jnp.bfloat16),
            pltpu.VMEM((2, half, 2 * LANES, 2 * LANES), jnp.bfloat16),
            pltpu.VMEM((2, comps, SUB, LANES), jnp.float32),
            pltpu.VMEM((2, comps, SUB, LANES), jnp.float32),
            dma, dma((3,)), dma((2,)), dma((2,)), dma((2,)), dma((2,)),
            dma((lon_count, chunks)), dma((lon_count, chunks)),
            dma((lon_count, chunks)), dma((lon_count, chunks)), dma((2, chunks)),
        ],
        compiler_params=pltpu.CompilerParams(
            collective_id=0, has_side_effects=True, vmem_limit_bytes=48 * 1024 * 1024
        ),
    )(state_now, geo, cut, wave, fwd, inv)
    return state_old + step_scale * filtered


def chunk_rows(share):
    for parts in (3, 2, 4, 1):
        if share % (parts * SUB) == 0:
            return share // parts
    return 0


def solution(mesh):
    lat_count, lon_count = mesh.shape["lat"], mesh.shape["lon"]

    def step(state_now, state_old, polar_cutoff):
        comps, lat_total, lon_total = state_now.shape
        rows, cols = lat_total // lat_count, lon_total // lon_count
        share = rows // lon_count
        fits = (
            lat_count >= 4 and lat_total == 4 * rows and rows % lon_count == 0
            and share % SUB == 0 and cols % (LANES // 2) == 0 and rows // SUB <= LANES
            and lon_total % (2 * LANES) == 0 and comps == 3 * mesh.shape["ens"]
        )
        body = per_device
        if fits:
            fwd, inv, wave = spectral_tables(lon_total)
            tables = (geometry_table(lat_total, lon_total), fwd, inv, wave)
            body = functools.partial(fused_step, (lat_count, lon_count), tables)
        return jax.shard_map(
            body,
            mesh=mesh,
            in_specs=(P("ens", "lat", "lon"), P("ens", "lat", "lon"), P()),
            out_specs=P("ens", "lat", "lon"),
            check_vma=False,
        )(state_now, state_old, polar_cutoff)

    return step
```

```python
import functools
import math

import jax
import jax.numpy as jnp
import numpy as np
from jax import lax
from jax.experimental import pallas as pl
from jax.experimental.pallas import tpu as pltpu
from jax.sharding import PartitionSpec as P

LANES = 128
SUB = 8
MESH = pl.DeviceIdType.MESH
step_scale = 0.2
coriolis = 2.0
gravity = 1.0
highest = lax.Precision.HIGHEST


def padded(value, sides, width, wrap):
    for axis, dim in sides:
        devices, length = (lax.axis_size(axis), value.shape[dim])
        up = [(i, (i + 1) % devices) for i in range(devices if wrap else devices - 1)]
        down = [(j, i) for i, j in up]
        last = lax.slice_in_dim(value, length - width, length, axis=dim)
        leading = lax.slice_in_dim(value, 0, width, axis=dim)
        before = lax.ppermute(last, axis, up)
        after = lax.ppermute(leading, axis, down)
        value = jnp.concatenate([before, value, after], axis=dim)
    return value


def latitude_terms(row_index, lat_total):
    distance = jnp.minimum(row_index + 0.5, lat_total - row_index - 0.5)
    cosine_lat = jnp.sin(math.pi * distance / lat_total)
    sine_lat = -jnp.cos(math.pi * (row_index + 0.5) / lat_total)
    return (cosine_lat, sine_lat)


def tendencies(lat_padded, lon_padded, cos_ext, sine_lat, lat_total, lon_total):
    cosine_lat = cos_ext[1:-1]
    zonal_scale = (lon_total / (4.0 * lat_total) / cosine_lat)[:, None]
    metric = math.pi / lat_total * sine_lat / cosine_lat
    depth_lon, east_lon, north_lon = (lon_padded[0], lon_padded[1], lon_padded[2])
    depth_lat, east_lat, north_lat = (lat_padded[0], lat_padded[1], lat_padded[2])
    east = east_lon[:, 1:-1]
    north = north_lon[:, 1:-1]

    def zonal_change(field):
        return zonal_scale * (field[:, 2:] - field[:, :-2])

    def northward_change(field):
        return 0.5 * (field[2:] - field[:-2])

    mass_flux = depth_lat * north_lat * cos_ext[:, None]
    tend_depth = (
        -zonal_change(depth_lon * east_lon) - northward_change(mass_flux) / cosine_lat[:, None]
    )
    turning = coriolis * sine_lat[:, None] + metric[:, None] * east
    tend_east = (
        -east * zonal_change(east_lon)
        - north * northward_change(east_lat)
        + turning * north
        - gravity * zonal_change(depth_lon)
    )
    tend_north = (
        -east * zonal_change(north_lon)
        - north * northward_change(north_lat)
        - turning * east
        - gravity * northward_change(depth_lat)
    )
    return jnp.stack([tend_depth, tend_east, tend_north])


def angle_table(first_count, second_count, period):
    first_idx = jnp.arange(first_count, dtype=jnp.int32)
    second_idx = jnp.arange(second_count, dtype=jnp.int32)
    turns = first_idx[:, None] * second_idx[None, :] % period
    phase = turns.astype(jnp.float32) * (2.0 * math.pi / period)
    return (jnp.cos(phase), jnp.sin(phase))


def low_pass(signal, cutoff):
    count, length = signal.shape
    first = 1
    probe = 1
    while probe * probe <= length:
        if length % probe == 0:
            first = probe
        probe = probe + 1
    second = length // first
    cos_first, sin_first = angle_table(first, first, first)
    cos_second, sin_second = angle_table(second, second, second)
    cos_twist, sin_twist = angle_table(first, second, length)
    grid = signal.reshape(count, first, second)
    part_re = jnp.einsum("cpq,pk->ckq", grid, cos_first, precision=highest)
    part_im = -jnp.einsum("cpq,pk->ckq", grid, sin_first, precision=highest)
    twist_re = part_re * cos_twist + part_im * sin_twist
    twist_im = part_im * cos_twist - part_re * sin_twist
    spec_re = jnp.einsum("ckq,qm->ckm", twist_re, cos_second, precision=highest) + jnp.einsum(
        "ckq,qm->ckm", twist_im, sin_second, precision=highest
    )
    spec_im = jnp.einsum("ckq,qm->ckm", twist_im, cos_second, precision=highest) - jnp.einsum(
        "ckq,qm->ckm", twist_re, sin_second, precision=highest
    )
    wave = (
        jnp.arange(first, dtype=jnp.int32)[:, None]
        + first * jnp.arange(second, dtype=jnp.int32)[None, :]
    )
    limit = cutoff[:, None, None]
    keep = ((wave[None] <= limit) | (wave[None] >= length - limit)).astype(jnp.float32) * (
        1.0 / length
    )
    spec_re = spec_re * keep
    spec_im = spec_im * keep
    back_re = jnp.einsum("ckm,mq->ckq", spec_re, cos_second, precision=highest) - jnp.einsum(
        "ckm,mq->ckq", spec_im, sin_second, precision=highest
    )
    back_im = jnp.einsum("ckm,mq->ckq", spec_im, cos_second, precision=highest) + jnp.einsum(
        "ckm,mq->ckq", spec_re, sin_second, precision=highest
    )
    turn_re = back_re * cos_twist - back_im * sin_twist
    turn_im = back_im * cos_twist + back_re * sin_twist
    result = jnp.einsum("ckq,kp->cpq", turn_re, cos_first, precision=highest) - jnp.einsum(
        "ckq,kp->cpq", turn_im, sin_first, precision=highest
    )
    return result.reshape(count, length)


def per_device(state_now, state_old, polar_cutoff):
    lat_rows = state_now.shape[1]
    lon_cols = state_now.shape[2]
    lat_count = lax.axis_size("lat")
    lon_count = lax.axis_size("lon")
    lat_total = lat_rows * lat_count
    lon_total = lon_cols * lon_count
    lat_place = lax.axis_index("lat")
    lat_padded = padded(state_now, (("lat", 1),), 1, False)
    lon_padded = padded(state_now, (("lon", 2),), 1, True)
    row_index = (lat_place * lat_rows + jnp.arange(-1, lat_rows + 1, dtype=jnp.int32)).astype(
        jnp.float32
    )
    cos_ext, sin_ext = latitude_terms(row_index, lat_total)
    forcing = tendencies(lat_padded, lon_padded, cos_ext, sin_ext[1:-1], lat_total, lon_total)
    groups = lat_count * lon_count
    share = lat_rows // groups
    member = lax.axis_index(("lat", "lon"))
    south_cut = lax.dynamic_slice_in_dim(polar_cutoff, member * share, share)
    north_cut = lax.dynamic_slice_in_dim(polar_cutoff, lat_rows + member * share, share)
    band_cut = jnp.concatenate([south_cut, north_cut])
    block = lax.all_to_all(forcing, ("lat", "lon"), split_axis=1, concat_axis=2, tiled=True)
    items = block.shape[0]
    wide = block.shape[2]
    south_rows = block[:, :, :lon_total]
    north_rows = block[:, :, wide - lon_total :]
    polar_rows = jnp.concatenate([south_rows, north_rows], axis=1)
    smooth = low_pass(polar_rows.reshape(items * 2 * share, lon_total), jnp.tile(band_cut, items))
    smooth = smooth.reshape(items, 2 * share, lon_total)
    rebuilt = jnp.concatenate(
        [smooth[:, :share], block[:, :, lon_total : wide - lon_total], smooth[:, share:]], axis=2
    )
    filtered = lax.all_to_all(rebuilt, ("lat", "lon"), split_axis=2, concat_axis=1, tiled=True)
    return state_old + step_scale * filtered


def spectral_tables(total):
    tiles = total // LANES
    half = tiles // 2
    q = np.arange(LANES)[:, None]
    m = np.arange(LANES)[None, :]
    forward = np.zeros((half, 2 * LANES, 2 * LANES))
    wave = np.zeros((half, 2 * LANES), np.int64)

    def angle(k):
        return 2.0 * np.pi * ((q * k) % total) / total

    mid = LANES // 2
    re_m = np.arange(mid + 1)[None, :]
    im_m = np.arange(1, mid)[None, :]
    k_re, k_im = tiles * re_m, tiles * im_m
    forward[0, :LANES, : mid + 1] = np.cos(angle(k_re))
    forward[0, :LANES, mid + 1 : LANES] = -np.sin(angle(k_im))
    k_odd = half + tiles * np.arange(mid)[None, :]
    odd = np.concatenate([np.cos(angle(k_odd)), -np.sin(angle(k_odd))], axis=1)
    forward[0, LANES:, LANES:] = odd
    wave[0] = np.concatenate([k_re[0], k_im[0], k_odd[0], k_odd[0]])
    for r in range(1, half):
        k = r + tiles * m
        c, s = np.cos(angle(k)), np.sin(angle(k))
        forward[r] = np.block([[c, -s], [s, c]])
        wave[r] = np.concatenate([k[0], k[0]])
    wave = np.minimum(wave, total - wave)

    def split(a):
        a = a.astype(np.float32)
        hi = a.astype(jnp.bfloat16)
        lo = (a - hi.astype(np.float32)).astype(jnp.bfloat16)
        return np.stack([hi, lo])

    bins = np.zeros((half, SUB, 2 * LANES), np.float32)
    bins[:, 0] = wave
    bins[:, 1] = 2.0 / total
    bins[0, 1, [0, mid]] = 1.0 / total
    return split(forward), bins


def geometry_table(lat_total, lon_total):
    j = np.arange(lat_total, dtype=np.float64)

    def cosine(row):
        return np.sin(np.pi * np.minimum(row + 0.5, lat_total - row - 0.5) / lat_total)

    c = cosine(j)
    s = -np.cos(np.pi * (j + 0.5) / lat_total)
    table = np.zeros((lat_total, LANES))
    table[:, 0] = lon_total / (4.0 * lat_total * c)
    table[:, 1] = 0.5 * cosine(j + 1) / c
    table[:, 2] = 0.5 * cosine(j - 1) / c
    table[:, 3] = coriolis * s
    table[:, 4] = np.pi / lat_total * s / c
    return table.astype(np.float32)


def forward_radix(tile, tiles):
    half = tiles // 2
    x = [tile(p) for p in range(tiles)]
    even = [None] * (half + 1)
    odd = [None] * (half + 1)
    even[0], even[half] = x[0], x[half]
    for p in range(1, half):
        even[p] = x[p] + x[tiles - p]
        odd[p] = x[p] - x[tiles - p]
    re, im = [None] * (half + 1), [None] * (half + 1)
    for r in range(half // 2 + 1):
        e = parity_sum([(even[p], math.cos(2 * math.pi * p * r / tiles)) for p in range(0, half + 1, 2)])
        o = parity_sum([(even[p], math.cos(2 * math.pi * p * r / tiles)) for p in range(1, half + 1, 2)])
        re[r] = e + o
        re[half - r] = e - o
        if 0 < r:
            es = parity_sum([(odd[p], math.sin(2 * math.pi * p * r / tiles)) for p in range(2, half, 2)])
            os = parity_sum([(odd[p], math.sin(2 * math.pi * p * r / tiles)) for p in range(1, half, 2)])
            im[r] = -(es + os)
            im[half - r] = es - os
    return re, im


def parity_sum(terms):
    total = None
    for value, factor in terms:
        if abs(factor - 1.0) < 1e-12:
            term = value
        elif abs(factor + 1.0) < 1e-12:
            term = -value
        elif abs(factor) < 1e-12:
            continue
        else:
            term = value * np.float32(factor)
        total = term if total is None else total + term
    return total if total is not None else jnp.zeros_like(terms[0][0])


def inverse_radix(re, im, tiles):
    half = tiles // 2
    x = [None] * tiles
    for p in range(half // 2 + 1):
        ce = parity_sum([(re[r], math.cos(2 * math.pi * p * r / tiles)) for r in range(0, half + 1, 2)])
        co = parity_sum([(re[r], math.cos(2 * math.pi * p * r / tiles)) for r in range(1, half + 1, 2)])
        if p == 0:
            x[0] = ce + co
            x[half] = ce - co
            continue
        se = parity_sum([(im[r], math.sin(2 * math.pi * p * r / tiles)) for r in range(2, half, 2)])
        so = parity_sum([(im[r], math.sin(2 * math.pi * p * r / tiles)) for r in range(1, half, 2)])
        c, s = ce + co, se + so
        x[p] = c - s
        x[tiles - p] = c + s
        c, s = ce - co, so - se
        x[half - p] = c - s
        x[half + p] = c + s
    return x


def split_dot(value, table, r, transpose):
    hi = value.astype(jnp.bfloat16)
    lo = (value - hi.astype(jnp.float32)).astype(jnp.bfloat16)
    big, small = table[0, r], table[1, r]
    dims = (((1,), (1 if transpose else 0,)), ((), ()))

    def dot(a, b):
        return lax.dot_general(a, b, dims, preferred_element_type=jnp.float32)

    return dot(hi, big) + dot(lo, big) + dot(hi, small)


def step_kernel(
    lat_count, lon_count, chunk,
    x_hbm, geo_hbm, cut_hbm, bins_hbm, fwd_hbm, out_ref,
    xp, geo, cut_ref, bins, go, recv, ret, back, full, spec, fwd, col_send, col_recv,
    load_sem, table_sem, row_send_sem, row_recv_sem, col_send_sem, col_recv_sem,
    go_send, go_recv, back_send, back_recv,
):
    rows, cols = out_ref.shape[1], out_ref.shape[2]
    share = rows // lon_count
    chunks = share // chunk
    groups = rows // SUB
    tiles = lon_count * cols // LANES
    half = tiles // 2
    lat = lax.axis_index("lat")
    lon = lax.axis_index("lon")
    west = lax.rem(lon + lon_count - 1, lon_count)
    east = lax.rem(lon + 1, lon_count)
    polar = jnp.logical_or(lat == 0, lat == lat_count - 1)
    has_south = lat > 0
    has_north = lat < lat_count - 1

    load = pltpu.make_async_copy(x_hbm, xp.at[:, pl.ds(SUB, rows), :], load_sem)
    load.start()
    geo_load = pltpu.make_async_copy(
        geo_hbm.at[pl.ds(pl.multiple_of(lat * rows, SUB), rows), :], geo, table_sem.at[0]
    )
    geo_load.start()
    table_loads = [
        pltpu.make_async_copy(src, dst, table_sem.at[i + 1])
        for i, (src, dst) in enumerate([(fwd_hbm, fwd), (bins_hbm, bins), (cut_hbm, cut_ref)])
    ]
    for copy in table_loads:
        copy.start()

    barrier = pltpu.get_barrier_semaphore()
    for k in range(1, lon_count):
        pl.semaphore_signal(
            barrier, inc=1, device_id={"lon": lax.rem(lon + k, lon_count)}, device_id_type=MESH
        )

    @pl.when(has_south)
    def _():
        pl.semaphore_signal(barrier, inc=1, device_id={"lat": lat - 1}, device_id_type=MESH)

    @pl.when(has_north)
    def _():
        pl.semaphore_signal(barrier, inc=1, device_id={"lat": lat + 1}, device_id_type=MESH)

    load.wait()
    lane = lax.broadcasted_iota(jnp.int32, (SUB, LANES), 1)

    packed = [jnp.zeros((SUB, LANES), jnp.float32) for _ in range(6)]
    for g in range(groups):
        here = lane == g
        for c in range(3):
            block = slice(SUB + g * SUB, 2 * SUB + g * SUB)
            packed[2 * c] = jnp.where(here, xp[c, block, 0:1], packed[2 * c])
            packed[2 * c + 1] = jnp.where(here, xp[c, block, cols - 1 : cols], packed[2 * c + 1])
    for c in range(3):
        col_send[0, c] = packed[2 * c]
        col_send[1, c] = packed[2 * c + 1]

    pl.semaphore_wait(
        barrier, lon_count - 1 + has_south.astype(jnp.int32) + has_north.astype(jnp.int32)
    )

    def to_south():
        return pltpu.make_async_remote_copy(
            src_ref=x_hbm.at[:, pl.ds(0, SUB), :], dst_ref=xp.at[:, pl.ds(rows + SUB, SUB), :],
            send_sem=row_send_sem.at[0], recv_sem=row_recv_sem.at[0],
            device_id={"lat": lat - 1}, device_id_type=MESH,
        )

    def to_north():
        return pltpu.make_async_remote_copy(
            src_ref=x_hbm.at[:, pl.ds(rows - SUB, SUB), :], dst_ref=xp.at[:, pl.ds(0, SUB), :],
            send_sem=row_send_sem.at[1], recv_sem=row_recv_sem.at[1],
            device_id={"lat": lat + 1}, device_id_type=MESH,
        )

    @pl.when(has_south)
    def _():
        to_south().start()

    @pl.when(has_north)
    def _():
        to_north().start()

    zero_rows = jnp.zeros((3, SUB, cols), jnp.float32)

    @pl.when(jnp.logical_not(has_south))
    def _():
        xp[:, 0:SUB, :] = zero_rows

    @pl.when(jnp.logical_not(has_north))
    def _():
        xp[:, rows + SUB : rows + 2 * SUB, :] = zero_rows

    def column_copy(side, target):
        return pltpu.make_async_remote_copy(
            src_ref=col_send.at[side], dst_ref=col_recv.at[side],
            send_sem=col_send_sem.at[side], recv_sem=col_recv_sem.at[side],
            device_id={"lon": target}, device_id_type=MESH,
        )

    first_out = column_copy(0, west)
    last_out = column_copy(1, east)
    first_out.start()
    last_out.start()
    geo_load.wait()
    first_out.wait()
    last_out.wait()

    @pl.when(has_south)
    def _():
        to_south().wait_send()
        to_north().wait_recv()

    @pl.when(has_north)
    def _():
        to_north().wait_send()
        to_south().wait_recv()

    sub_idx = lax.broadcasted_iota(jnp.int32, (SUB, cols), 0)

    def tendency_group(g):
        start = pl.multiple_of(g * SUB, SUB)
        terms = geo[pl.ds(start, SUB), :]
        zonal, up, down, turn, metric = [terms[:, i : i + 1] for i in range(5)]
        cur, north, south, diff, east_of, west_of = [], [], [], [], [], []
        for c in range(3):
            before = xp[c, pl.ds(start, SUB), :]
            here = xp[c, pl.ds(pl.multiple_of(start + SUB, SUB), SUB), :]
            after = xp[c, pl.ds(pl.multiple_of(start + 2 * SUB, SUB), SUB), :]
            north.append(pltpu.roll(jnp.where(sub_idx == 0, after, here), SUB - 1, 0))
            south.append(pltpu.roll(jnp.where(sub_idx == SUB - 1, before, here), 1, 0))
            on = lane == g
            right = jnp.sum(jnp.where(on, col_recv[0, c], 0.0), axis=1, keepdims=True)
            left = jnp.sum(jnp.where(on, col_recv[1, c], 0.0), axis=1, keepdims=True)
            east_of.append(jnp.concatenate([here[:, 1:], right], axis=1))
            west_of.append(jnp.concatenate([left, here[:, :-1]], axis=1))
            cur.append(here)
        h, u, v = cur
        t_h = -zonal * (east_of[0] * east_of[1] - west_of[0] * west_of[1]) - (
            up * (north[0] * north[2]) - down * (south[0] * south[2])
        )
        turning = turn + metric * u
        zu = zonal * u
        hv = 0.5 * v
        t_u = (
            turning * v - zu * (east_of[1] - west_of[1]) - hv * (north[1] - south[1])
            - zonal * (east_of[0] - west_of[0])
        )
        t_v = (
            -turning * u - zu * (east_of[2] - west_of[2]) - hv * (north[2] - south[2])
            - 0.5 * (north[0] - south[0])
        )
        return t_h, t_u, t_v

    def aligned(i):
        return pl.multiple_of(i, SUB)

    per_chunk = chunk // SUB
    whole = cols // LANES
    half_at = whole * 3 * chunk

    def half_place(group):
        return pl.ds(half_at + group // 2 * SUB, SUB), pl.ds(group % 2 * (LANES // 2), LANES // 2)

    def go_copy(part, target, source):
        return pltpu.make_async_remote_copy(
            src_ref=go.at[target, part], dst_ref=recv.at[source, part],
            send_sem=go_send.at[target, part], recv_sem=go_recv.at[source, part],
            device_id={"lon": target}, device_id_type=MESH,
        )

    def back_copy(part, target, source):
        return pltpu.make_async_remote_copy(
            src_ref=ret.at[target, part], dst_ref=back.at[source, part],
            send_sem=back_send.at[target, part], recv_sem=back_recv.at[source, part],
            device_id={"lon": target}, device_id_type=MESH,
        )

    def make_piece(buf, place, part, target):
        first = (target * share + part * chunk) // SUB
        for i in range(per_chunk):
            values = tendency_group(first + i)
            for c in range(3):
                group = c * per_chunk + i
                for t in range(whole):
                    buf[place, part, t * 3 * chunk + group * SUB : t * 3 * chunk + (group + 1) * SUB, :] = (
                        values[c][:, t * LANES : (t + 1) * LANES]
                    )
                if cols % LANES:
                    at_rows, at_lanes = half_place(group)
                    buf[place, part, at_rows, at_lanes] = values[c][:, whole * LANES :]

    def unpack(buf, part, source):
        first = source * share + part * chunk
        for c in range(3):
            for t in range(whole):
                out_ref[c, pl.ds(aligned(first), chunk), t * LANES : (t + 1) * LANES] = buf[
                    source, part, pl.ds((t * 3 + c) * chunk, chunk), :
                ]
            if cols % LANES:
                for i in range(per_chunk):
                    at_rows, at_lanes = half_place(c * per_chunk + i)
                    out_ref[c, pl.ds(aligned(first + i * SUB), SUB), whole * LANES :] = buf[
                        source, part, at_rows, at_lanes
                    ]

    @pl.when(polar)
    def _():
        @pl.loop(0, chunks)
        def _(part):
            @pl.loop(1, lon_count)
            def _(k):
                target = lax.rem(lon + k, lon_count)
                make_piece(go, target, part, target)
                go_copy(part, target, lon).start()

            make_piece(recv, lon, part, lon)

    @pl.when(jnp.logical_not(polar))
    def _():
        @pl.loop(0, groups)
        def _(g):
            values = tendency_group(g)
            for c in range(3):
                out_ref[c, pl.ds(aligned(g * SUB), SUB), :] = values[c]

    for copy in table_loads:
        copy.wait()

    cut_start = jnp.where(lat == 0, 0, rows) + lon * share

    @pl.when(polar)
    def _():
        @pl.loop(0, chunks)
        def _(part):
            for k in range(1, lon_count):
                go_copy(part, lon, lax.rem(lon + k, lon_count)).wait_recv()
            for d in range(lon_count):
                for t in range(whole):
                    lanes = slice(d * cols + t * LANES, d * cols + (t + 1) * LANES)
                    full[:, lanes] = recv[d, part, t * 3 * chunk : (t + 1) * 3 * chunk, :]
                if cols % LANES:
                    lanes = slice(d * cols + whole * LANES, (d + 1) * cols)
                    for group in range(3 * per_chunk):
                        at_rows, at_lanes = half_place(group)
                        full[group * SUB : (group + 1) * SUB, lanes] = recv[d, part, at_rows, at_lanes]

            @pl.loop(0, 3 * chunk // SUB)
            def _(g):
                block = pl.ds(aligned(g * SUB), SUB)
                re, im = forward_radix(lambda p: full[block, p * LANES : (p + 1) * LANES], tiles)
                spec[0, block, :LANES] = re[0]
                spec[0, block, LANES:] = re[half]
                for r in range(1, half):
                    spec[r, block, :LANES] = re[r]
                    spec[r, block, LANES:] = im[r]

            wanted = cut_start + part * chunk + lax.broadcasted_iota(jnp.int32, (chunk, 2 * rows), 0)
            hit = wanted == lax.broadcasted_iota(jnp.int32, (chunk, 2 * rows), 1)
            cuts = cut_ref[0:1, :].astype(jnp.float32)
            limit = jnp.sum(jnp.where(hit, cuts, 0.0), axis=1, keepdims=True)
            limit = jnp.concatenate([limit, limit, limit], axis=0)

            @pl.loop(0, half)
            def _(r):
                z = split_dot(spec[r], fwd, r, False)
                z = jnp.where(bins[r, 0:1, :] <= limit, z * bins[r, 1:2, :], 0.0)
                spec[r] = split_dot(z, fwd, r, True)

            @pl.loop(0, 3 * chunk // SUB)
            def _(g):
                block = pl.ds(aligned(g * SUB), SUB)
                re = [spec[r, block, :LANES] for r in range(half)] + [spec[0, block, LANES:]]
                im = [None] + [spec[r, block, LANES:] for r in range(1, half)]
                x = inverse_radix(re, im, tiles)
                for p in range(tiles):
                    full[block, p * LANES : (p + 1) * LANES] = x[p]

            for d in range(lon_count):
                for t in range(whole):
                    lanes = slice(d * cols + t * LANES, d * cols + (t + 1) * LANES)
                    ret[d, part, t * 3 * chunk : (t + 1) * 3 * chunk, :] = full[:, lanes]
                if cols % LANES:
                    lanes = slice(d * cols + whole * LANES, (d + 1) * cols)
                    for group in range(3 * per_chunk):
                        at_rows, at_lanes = half_place(group)
                        ret[d, part, at_rows, at_lanes] = full[group * SUB : (group + 1) * SUB, lanes]
            for k in range(1, lon_count):
                back_copy(part, lax.rem(lon + k, lon_count), lon).start()
            unpack(ret, part, lon)

        @pl.loop(0, chunks)
        def _(part):
            @pl.loop(1, lon_count)
            def _(k):
                other = lax.rem(lon + k, lon_count)
                go_copy(part, other, lon).wait_send()
                back_copy(part, lon, other).wait_recv()
                unpack(back, part, other)
                back_copy(part, other, lon).wait_send()


def fused_step(mesh_shape, tables, state_now, state_old, polar_cutoff):
    lat_count, lon_count = mesh_shape
    comps, rows, cols = state_now.shape
    share = rows // lon_count
    total = lon_count * cols
    half = total // LANES // 2
    chunk = chunk_rows(share)
    chunks = share // chunk
    geo, fwd, bins = tables
    groups = comps * chunk // SUB
    piece = (cols // LANES * groups + (groups + 1) // 2 * (cols % LANES > 0)) * SUB
    operands = [
        pltpu.with_memory_space_constraint(jnp.asarray(a), pltpu.HBM)
        for a in (state_now, geo, polar_cutoff.reshape(1, 2 * rows), bins, fwd)
    ]
    hbm_spec = pl.BlockSpec(memory_space=pltpu.HBM)
    vmem_spec = pl.BlockSpec(memory_space=pltpu.VMEM)
    dma = pltpu.SemaphoreType.DMA
    filtered = pl.pallas_call(
        functools.partial(step_kernel, lat_count, lon_count, chunk),
        out_shape=jax.ShapeDtypeStruct(state_now.shape, jnp.float32),
        in_specs=[hbm_spec] * 5,
        out_specs=vmem_spec,
        scratch_shapes=[
            pltpu.VMEM((comps, rows + 2 * SUB, cols), jnp.float32),
            pltpu.VMEM((rows, LANES), jnp.float32),
            pltpu.VMEM((1, 2 * rows), jnp.int32),
            pltpu.VMEM((half, SUB, 2 * LANES), jnp.float32),
            pltpu.VMEM((lon_count, chunks, piece, LANES), jnp.float32),
            pltpu.VMEM((lon_count, chunks, piece, LANES), jnp.float32),
            pltpu.VMEM((lon_count, chunks, piece, LANES), jnp.float32),
            pltpu.VMEM((lon_count, chunks, piece, LANES), jnp.float32),
            pltpu.VMEM((comps * chunk, total), jnp.float32),
            pltpu.VMEM((half, comps * chunk, 2 * LANES), jnp.float32),
            pltpu.VMEM((2, half, 2 * LANES, 2 * LANES), jnp.bfloat16),
            pltpu.VMEM((2, comps, SUB, LANES), jnp.float32),
            pltpu.VMEM((2, comps, SUB, LANES), jnp.float32),
            dma, dma((4,)), dma((2,)), dma((2,)), dma((2,)), dma((2,)),
            dma((lon_count, chunks)), dma((lon_count, chunks)),
            dma((lon_count, chunks)), dma((lon_count, chunks)),
        ],
        compiler_params=pltpu.CompilerParams(
            collective_id=0, has_side_effects=True, vmem_limit_bytes=48 * 1024 * 1024
        ),
    )(*operands)
    return state_old + step_scale * filtered


def chunk_rows(share):
    for parts in (3, 2, 4, 1):
        if share % (parts * SUB) == 0:
            return share // parts
    return 0


def solution(mesh):
    lat_count, lon_count = mesh.shape["lat"], mesh.shape["lon"]

    def step(state_now, state_old, polar_cutoff):
        comps, lat_total, lon_total = state_now.shape
        rows, cols = lat_total // lat_count, lon_total // lon_count
        share = rows // lon_count
        fits = (
            lat_count >= 4 and lat_total == 4 * rows and rows % lon_count == 0
            and share % SUB == 0 and cols % (LANES // 2) == 0 and rows // SUB <= LANES
            and lon_total % (2 * LANES) == 0 and comps == 3 * mesh.shape["ens"]
        )
        body = per_device
        if fits:
            tables = (geometry_table(lat_total, lon_total), *spectral_tables(lon_total))
            body = functools.partial(fused_step, (lat_count, lon_count), tables)
        return jax.shard_map(
            body,
            mesh=mesh,
            in_specs=(P("ens", "lat", "lon"), P("ens", "lat", "lon"), P()),
            out_specs=P("ens", "lat", "lon"),
            check_vma=False,
        )(state_now, state_old, polar_cutoff)

    return step
```

```python
import functools
import math

import jax
import jax.numpy as jnp
import numpy as np
from jax import lax
from jax.experimental import pallas as pl
from jax.experimental.pallas import tpu as pltpu
from jax.sharding import PartitionSpec as P

LANES = 128
SUB = 8
MESH = pl.DeviceIdType.MESH
step_scale = 0.2
coriolis = 2.0
gravity = 1.0
highest = lax.Precision.HIGHEST


def padded(value, sides, width, wrap):
    for axis, dim in sides:
        devices, length = (lax.axis_size(axis), value.shape[dim])
        up = [(i, (i + 1) % devices) for i in range(devices if wrap else devices - 1)]
        down = [(j, i) for i, j in up]
        last = lax.slice_in_dim(value, length - width, length, axis=dim)
        leading = lax.slice_in_dim(value, 0, width, axis=dim)
        before = lax.ppermute(last, axis, up)
        after = lax.ppermute(leading, axis, down)
        value = jnp.concatenate([before, value, after], axis=dim)
    return value


def latitude_terms(row_index, lat_total):
    distance = jnp.minimum(row_index + 0.5, lat_total - row_index - 0.5)
    cosine_lat = jnp.sin(math.pi * distance / lat_total)
    sine_lat = -jnp.cos(math.pi * (row_index + 0.5) / lat_total)
    return (cosine_lat, sine_lat)


def tendencies(lat_padded, lon_padded, cos_ext, sine_lat, lat_total, lon_total):
    cosine_lat = cos_ext[1:-1]
    zonal_scale = (lon_total / (4.0 * lat_total) / cosine_lat)[:, None]
    metric = math.pi / lat_total * sine_lat / cosine_lat
    depth_lon, east_lon, north_lon = (lon_padded[0], lon_padded[1], lon_padded[2])
    depth_lat, east_lat, north_lat = (lat_padded[0], lat_padded[1], lat_padded[2])
    east = east_lon[:, 1:-1]
    north = north_lon[:, 1:-1]

    def zonal_change(field):
        return zonal_scale * (field[:, 2:] - field[:, :-2])

    def northward_change(field):
        return 0.5 * (field[2:] - field[:-2])

    mass_flux = depth_lat * north_lat * cos_ext[:, None]
    tend_depth = (
        -zonal_change(depth_lon * east_lon) - northward_change(mass_flux) / cosine_lat[:, None]
    )
    turning = coriolis * sine_lat[:, None] + metric[:, None] * east
    tend_east = (
        -east * zonal_change(east_lon)
        - north * northward_change(east_lat)
        + turning * north
        - gravity * zonal_change(depth_lon)
    )
    tend_north = (
        -east * zonal_change(north_lon)
        - north * northward_change(north_lat)
        - turning * east
        - gravity * northward_change(depth_lat)
    )
    return jnp.stack([tend_depth, tend_east, tend_north])


def angle_table(first_count, second_count, period):
    first_idx = jnp.arange(first_count, dtype=jnp.int32)
    second_idx = jnp.arange(second_count, dtype=jnp.int32)
    turns = first_idx[:, None] * second_idx[None, :] % period
    phase = turns.astype(jnp.float32) * (2.0 * math.pi / period)
    return (jnp.cos(phase), jnp.sin(phase))


def low_pass(signal, cutoff):
    count, length = signal.shape
    first = 1
    probe = 1
    while probe * probe <= length:
        if length % probe == 0:
            first = probe
        probe = probe + 1
    second = length // first
    cos_first, sin_first = angle_table(first, first, first)
    cos_second, sin_second = angle_table(second, second, second)
    cos_twist, sin_twist = angle_table(first, second, length)
    grid = signal.reshape(count, first, second)
    part_re = jnp.einsum("cpq,pk->ckq", grid, cos_first, precision=highest)
    part_im = -jnp.einsum("cpq,pk->ckq", grid, sin_first, precision=highest)
    twist_re = part_re * cos_twist + part_im * sin_twist
    twist_im = part_im * cos_twist - part_re * sin_twist
    spec_re = jnp.einsum("ckq,qm->ckm", twist_re, cos_second, precision=highest) + jnp.einsum(
        "ckq,qm->ckm", twist_im, sin_second, precision=highest
    )
    spec_im = jnp.einsum("ckq,qm->ckm", twist_im, cos_second, precision=highest) - jnp.einsum(
        "ckq,qm->ckm", twist_re, sin_second, precision=highest
    )
    wave = (
        jnp.arange(first, dtype=jnp.int32)[:, None]
        + first * jnp.arange(second, dtype=jnp.int32)[None, :]
    )
    limit = cutoff[:, None, None]
    keep = ((wave[None] <= limit) | (wave[None] >= length - limit)).astype(jnp.float32) * (
        1.0 / length
    )
    spec_re = spec_re * keep
    spec_im = spec_im * keep
    back_re = jnp.einsum("ckm,mq->ckq", spec_re, cos_second, precision=highest) - jnp.einsum(
        "ckm,mq->ckq", spec_im, sin_second, precision=highest
    )
    back_im = jnp.einsum("ckm,mq->ckq", spec_im, cos_second, precision=highest) + jnp.einsum(
        "ckm,mq->ckq", spec_re, sin_second, precision=highest
    )
    turn_re = back_re * cos_twist - back_im * sin_twist
    turn_im = back_im * cos_twist + back_re * sin_twist
    result = jnp.einsum("ckq,kp->cpq", turn_re, cos_first, precision=highest) - jnp.einsum(
        "ckq,kp->cpq", turn_im, sin_first, precision=highest
    )
    return result.reshape(count, length)


def per_device(state_now, state_old, polar_cutoff):
    lat_rows = state_now.shape[1]
    lon_cols = state_now.shape[2]
    lat_count = lax.axis_size("lat")
    lon_count = lax.axis_size("lon")
    lat_total = lat_rows * lat_count
    lon_total = lon_cols * lon_count
    lat_place = lax.axis_index("lat")
    lat_padded = padded(state_now, (("lat", 1),), 1, False)
    lon_padded = padded(state_now, (("lon", 2),), 1, True)
    row_index = (lat_place * lat_rows + jnp.arange(-1, lat_rows + 1, dtype=jnp.int32)).astype(
        jnp.float32
    )
    cos_ext, sin_ext = latitude_terms(row_index, lat_total)
    forcing = tendencies(lat_padded, lon_padded, cos_ext, sin_ext[1:-1], lat_total, lon_total)
    groups = lat_count * lon_count
    share = lat_rows // groups
    member = lax.axis_index(("lat", "lon"))
    south_cut = lax.dynamic_slice_in_dim(polar_cutoff, member * share, share)
    north_cut = lax.dynamic_slice_in_dim(polar_cutoff, lat_rows + member * share, share)
    band_cut = jnp.concatenate([south_cut, north_cut])
    block = lax.all_to_all(forcing, ("lat", "lon"), split_axis=1, concat_axis=2, tiled=True)
    items = block.shape[0]
    wide = block.shape[2]
    south_rows = block[:, :, :lon_total]
    north_rows = block[:, :, wide - lon_total :]
    polar_rows = jnp.concatenate([south_rows, north_rows], axis=1)
    smooth = low_pass(polar_rows.reshape(items * 2 * share, lon_total), jnp.tile(band_cut, items))
    smooth = smooth.reshape(items, 2 * share, lon_total)
    rebuilt = jnp.concatenate(
        [smooth[:, :share], block[:, :, lon_total : wide - lon_total], smooth[:, share:]], axis=2
    )
    filtered = lax.all_to_all(rebuilt, ("lat", "lon"), split_axis=2, concat_axis=1, tiled=True)
    return state_old + step_scale * filtered


def spectral_tables(total):
    tiles = total // LANES
    half = tiles // 2
    q = np.arange(LANES)[:, None]
    m = np.arange(LANES)[None, :]
    forward = np.zeros((half, 2 * LANES, 2 * LANES))
    wave = np.zeros((half, 2 * LANES), np.int64)

    def angle(k):
        return 2.0 * np.pi * ((q * k) % total) / total

    mid = LANES // 2
    re_m = np.arange(mid + 1)[None, :]
    im_m = np.arange(1, mid)[None, :]
    k_re, k_im = tiles * re_m, tiles * im_m
    forward[0, :LANES, : mid + 1] = np.cos(angle(k_re))
    forward[0, :LANES, mid + 1 : LANES] = -np.sin(angle(k_im))
    k_odd = half + tiles * np.arange(mid)[None, :]
    odd = np.concatenate([np.cos(angle(k_odd)), -np.sin(angle(k_odd))], axis=1)
    forward[0, LANES:, LANES:] = odd
    wave[0] = np.concatenate([k_re[0], k_im[0], k_odd[0], k_odd[0]])
    for r in range(1, half):
        k = r + tiles * m
        c, s = np.cos(angle(k)), np.sin(angle(k))
        forward[r] = np.block([[c, -s], [s, c]])
        wave[r] = np.concatenate([k[0], k[0]])
    wave = np.minimum(wave, total - wave)

    def split(a):
        a = a.astype(np.float32)
        hi = a.astype(jnp.bfloat16)
        lo = (a - hi.astype(np.float32)).astype(jnp.bfloat16)
        return np.stack([hi, lo])

    bins = np.zeros((half, SUB, 2 * LANES), np.float32)
    bins[:, 0] = wave
    bins[:, 1] = 2.0 / total
    bins[0, 1, [0, mid]] = 1.0 / total
    return split(forward), bins


def geometry_table(lat_total, lon_total):
    j = np.arange(lat_total, dtype=np.float64)

    def cosine(row):
        return np.sin(np.pi * np.minimum(row + 0.5, lat_total - row - 0.5) / lat_total)

    c = cosine(j)
    s = -np.cos(np.pi * (j + 0.5) / lat_total)
    table = np.zeros((lat_total, LANES))
    table[:, 0] = lon_total / (4.0 * lat_total * c)
    table[:, 1] = 0.5 * cosine(j + 1) / c
    table[:, 2] = 0.5 * cosine(j - 1) / c
    table[:, 3] = coriolis * s
    table[:, 4] = np.pi / lat_total * s / c
    return table.astype(np.float32)


def forward_radix(tile, tiles):
    half = tiles // 2
    x = [tile(p) for p in range(tiles)]
    even = [None] * (half + 1)
    odd = [None] * (half + 1)
    even[0], even[half] = x[0], x[half]
    for p in range(1, half):
        even[p] = x[p] + x[tiles - p]
        odd[p] = x[p] - x[tiles - p]
    re, im = [None] * (half + 1), [None] * (half + 1)
    for r in range(half // 2 + 1):
        e = parity_sum([(even[p], math.cos(2 * math.pi * p * r / tiles)) for p in range(0, half + 1, 2)])
        o = parity_sum([(even[p], math.cos(2 * math.pi * p * r / tiles)) for p in range(1, half + 1, 2)])
        re[r] = e + o
        re[half - r] = e - o
        if 0 < r:
            es = parity_sum([(odd[p], math.sin(2 * math.pi * p * r / tiles)) for p in range(2, half, 2)])
            os = parity_sum([(odd[p], math.sin(2 * math.pi * p * r / tiles)) for p in range(1, half, 2)])
            im[r] = -(es + os)
            im[half - r] = es - os
    return re, im


def parity_sum(terms):
    total = None
    for value, factor in terms:
        if abs(factor - 1.0) < 1e-12:
            term = value
        elif abs(factor + 1.0) < 1e-12:
            term = -value
        elif abs(factor) < 1e-12:
            continue
        else:
            term = value * np.float32(factor)
        total = term if total is None else total + term
    return total if total is not None else jnp.zeros_like(terms[0][0])


def inverse_radix(re, im, tiles):
    half = tiles // 2
    x = [None] * tiles
    for p in range(half // 2 + 1):
        ce = parity_sum([(re[r], math.cos(2 * math.pi * p * r / tiles)) for r in range(0, half + 1, 2)])
        co = parity_sum([(re[r], math.cos(2 * math.pi * p * r / tiles)) for r in range(1, half + 1, 2)])
        if p == 0:
            x[0] = ce + co
            x[half] = ce - co
            continue
        se = parity_sum([(im[r], math.sin(2 * math.pi * p * r / tiles)) for r in range(2, half, 2)])
        so = parity_sum([(im[r], math.sin(2 * math.pi * p * r / tiles)) for r in range(1, half, 2)])
        c, s = ce + co, se + so
        x[p] = c - s
        x[tiles - p] = c + s
        c, s = ce - co, so - se
        x[half - p] = c - s
        x[half + p] = c + s
    return x


def split_dot(value, table, r, transpose):
    hi = value.astype(jnp.bfloat16)
    lo = (value - hi.astype(jnp.float32)).astype(jnp.bfloat16)
    big, small = table[0, r], table[1, r]
    dims = (((1,), (1 if transpose else 0,)), ((), ()))

    def dot(a, b):
        return lax.dot_general(a, b, dims, preferred_element_type=jnp.float32)

    return dot(hi, big) + dot(lo, big) + dot(hi, small)


def step_kernel(
    lat_count, lon_count, chunk,
    x_hbm, geo_hbm, cut_hbm, bins_hbm, fwd_hbm, out_ref,
    xp, geo, cut_ref, bins, go, recv, ret, back, full, spec, fwd, col_send, col_recv,
    load_sem, table_sem, row_send_sem, row_recv_sem, col_send_sem, col_recv_sem,
    go_send, go_recv, back_send, back_recv,
):
    rows, cols = out_ref.shape[1], out_ref.shape[2]
    share = rows // lon_count
    chunks = share // chunk
    groups = rows // SUB
    tiles = lon_count * cols // LANES
    half = tiles // 2
    lat = lax.axis_index("lat")
    lon = lax.axis_index("lon")
    west = lax.rem(lon + lon_count - 1, lon_count)
    east = lax.rem(lon + 1, lon_count)
    polar = jnp.logical_or(lat == 0, lat == lat_count - 1)
    has_south = lat > 0
    has_north = lat < lat_count - 1

    load = pltpu.make_async_copy(x_hbm, xp.at[:, pl.ds(SUB, rows), :], load_sem)
    load.start()
    geo_load = pltpu.make_async_copy(
        geo_hbm.at[pl.ds(pl.multiple_of(lat * rows, SUB), rows), :], geo, table_sem.at[0]
    )
    geo_load.start()
    table_loads = [
        pltpu.make_async_copy(src, dst, table_sem.at[i + 1])
        for i, (src, dst) in enumerate([(fwd_hbm, fwd), (bins_hbm, bins), (cut_hbm, cut_ref)])
    ]
    for copy in table_loads:
        copy.start()

    barrier = pltpu.get_barrier_semaphore()
    for k in range(1, lon_count):
        pl.semaphore_signal(
            barrier, inc=1, device_id={"lon": lax.rem(lon + k, lon_count)}, device_id_type=MESH
        )

    @pl.when(has_south)
    def _():
        pl.semaphore_signal(barrier, inc=1, device_id={"lat": lat - 1}, device_id_type=MESH)

    @pl.when(has_north)
    def _():
        pl.semaphore_signal(barrier, inc=1, device_id={"lat": lat + 1}, device_id_type=MESH)

    load.wait()
    lane = lax.broadcasted_iota(jnp.int32, (SUB, LANES), 1)

    packed = [jnp.zeros((SUB, LANES), jnp.float32) for _ in range(6)]
    for g in range(groups):
        here = lane == g
        for c in range(3):
            block = slice(SUB + g * SUB, 2 * SUB + g * SUB)
            packed[2 * c] = jnp.where(here, xp[c, block, 0:1], packed[2 * c])
            packed[2 * c + 1] = jnp.where(here, xp[c, block, cols - 1 : cols], packed[2 * c + 1])
    for c in range(3):
        col_send[0, c] = packed[2 * c]
        col_send[1, c] = packed[2 * c + 1]

    pl.semaphore_wait(
        barrier, lon_count - 1 + has_south.astype(jnp.int32) + has_north.astype(jnp.int32)
    )

    def to_south():
        return pltpu.make_async_remote_copy(
            src_ref=x_hbm.at[:, pl.ds(0, SUB), :], dst_ref=xp.at[:, pl.ds(rows + SUB, SUB), :],
            send_sem=row_send_sem.at[0], recv_sem=row_recv_sem.at[0],
            device_id={"lat": lat - 1}, device_id_type=MESH,
        )

    def to_north():
        return pltpu.make_async_remote_copy(
            src_ref=x_hbm.at[:, pl.ds(rows - SUB, SUB), :], dst_ref=xp.at[:, pl.ds(0, SUB), :],
            send_sem=row_send_sem.at[1], recv_sem=row_recv_sem.at[1],
            device_id={"lat": lat + 1}, device_id_type=MESH,
        )

    @pl.when(has_south)
    def _():
        to_south().start()

    @pl.when(has_north)
    def _():
        to_north().start()

    zero_rows = jnp.zeros((3, SUB, cols), jnp.float32)

    @pl.when(jnp.logical_not(has_south))
    def _():
        xp[:, 0:SUB, :] = zero_rows

    @pl.when(jnp.logical_not(has_north))
    def _():
        xp[:, rows + SUB : rows + 2 * SUB, :] = zero_rows

    def column_copy(side, target):
        return pltpu.make_async_remote_copy(
            src_ref=col_send.at[side], dst_ref=col_recv.at[side],
            send_sem=col_send_sem.at[side], recv_sem=col_recv_sem.at[side],
            device_id={"lon": target}, device_id_type=MESH,
        )

    first_out = column_copy(0, west)
    last_out = column_copy(1, east)
    first_out.start()
    last_out.start()
    geo_load.wait()
    sub_idx = lax.broadcasted_iota(jnp.int32, (SUB, cols), 0)

    def tendency_group(g, edges=True):
        start = pl.multiple_of(g * SUB, SUB)
        terms = geo[pl.ds(start, SUB), :]
        zonal, up, down, turn, metric = [terms[:, i : i + 1] for i in range(5)]
        cur, north, south, diff, east_of, west_of = [], [], [], [], [], []
        for c in range(3):
            before = xp[c, pl.ds(start, SUB), :]
            here = xp[c, pl.ds(pl.multiple_of(start + SUB, SUB), SUB), :]
            after = xp[c, pl.ds(pl.multiple_of(start + 2 * SUB, SUB), SUB), :]
            north.append(pltpu.roll(jnp.where(sub_idx == 0, after, here), SUB - 1, 0))
            south.append(pltpu.roll(jnp.where(sub_idx == SUB - 1, before, here), 1, 0))
            if edges:
                on = lane == g
                right = jnp.sum(jnp.where(on, col_recv[0, c], 0.0), axis=1, keepdims=True)
                left = jnp.sum(jnp.where(on, col_recv[1, c], 0.0), axis=1, keepdims=True)
            else:
                right, left = here[:, -1:], here[:, :1]
            east_of.append(jnp.concatenate([here[:, 1:], right], axis=1))
            west_of.append(jnp.concatenate([left, here[:, :-1]], axis=1))
            cur.append(here)
        h, u, v = cur
        t_h = -zonal * (east_of[0] * east_of[1] - west_of[0] * west_of[1]) - (
            up * (north[0] * north[2]) - down * (south[0] * south[2])
        )
        turning = turn + metric * u
        zu = zonal * u
        hv = 0.5 * v
        t_u = (
            turning * v - zu * (east_of[1] - west_of[1]) - hv * (north[1] - south[1])
            - zonal * (east_of[0] - west_of[0])
        )
        t_v = (
            -turning * u - zu * (east_of[2] - west_of[2]) - hv * (north[2] - south[2])
            - 0.5 * (north[0] - south[0])
        )
        return t_h, t_u, t_v

    def halos_arrive():
        first_out.wait()
        last_out.wait()

        @pl.when(has_south)
        def _():
            to_south().wait_send()
            to_north().wait_recv()

        @pl.when(has_north)
        def _():
            to_north().wait_send()
            to_south().wait_recv()

    def aligned(i):
        return pl.multiple_of(i, SUB)

    per_chunk = chunk // SUB
    whole = cols // LANES
    half_at = whole * 3 * chunk

    def half_place(group):
        return pl.ds(half_at + group // 2 * SUB, SUB), pl.ds(group % 2 * (LANES // 2), LANES // 2)

    inner = (whole - 1) * 3 * chunk
    piece = go.shape[2]

    def slot(tile):
        return ((tile + whole - 1) % whole) * 3 * chunk

    def go_copy(part, target, source, side):
        span = pl.ds(0, inner) if side == 0 else pl.ds(inner, piece - inner)
        return pltpu.make_async_remote_copy(
            src_ref=go.at[target, part, span, :], dst_ref=recv.at[source, part, span, :],
            send_sem=go_send.at[side, target, part], recv_sem=go_recv.at[side, source, part],
            device_id={"lon": target}, device_id_type=MESH,
        )

    def back_copy(part, target, source):
        return pltpu.make_async_remote_copy(
            src_ref=ret.at[target, part], dst_ref=back.at[source, part],
            send_sem=back_send.at[target, part], recv_sem=back_recv.at[source, part],
            device_id={"lon": target}, device_id_type=MESH,
        )

    def make_piece(buf, place, part, target, inside=True, outside=True):
        first = (target * share + part * chunk) // SUB
        for i in range(per_chunk):
            values = tendency_group(first + i, edges=outside)
            for c in range(3):
                group = c * per_chunk + i
                for t in range(whole):
                    if outside if t == 0 else inside:
                        buf[place, part, slot(t) + group * SUB : slot(t) + (group + 1) * SUB, :] = (
                            values[c][:, t * LANES : (t + 1) * LANES]
                        )
                if outside and cols % LANES:
                    at_rows, at_lanes = half_place(group)
                    buf[place, part, at_rows, at_lanes] = values[c][:, whole * LANES :]

    def unpack(buf, part, source):
        first = source * share + part * chunk
        for c in range(3):
            for t in range(whole):
                out_ref[c, pl.ds(aligned(first), chunk), t * LANES : (t + 1) * LANES] = buf[
                    source, part, pl.ds(slot(t) + c * chunk, chunk), :
                ]
            if cols % LANES:
                for i in range(per_chunk):
                    at_rows, at_lanes = half_place(c * per_chunk + i)
                    out_ref[c, pl.ds(aligned(first + i * SUB), SUB), whole * LANES :] = buf[
                        source, part, at_rows, at_lanes
                    ]

    def nth(i):
        return lax.rem(i + 1, chunks)

    @pl.when(polar)
    def _():
        @pl.loop(1, lon_count)
        def _(k):
            target = lax.rem(lon + k, lon_count)
            make_piece(go, target, nth(0), target, outside=False)
            go_copy(nth(0), target, lon, 0).start()

    halos_arrive()

    @pl.when(polar)
    def _():
        @pl.loop(1, lon_count)
        def _(k):
            target = lax.rem(lon + k, lon_count)
            make_piece(go, target, nth(0), target, inside=False)
            go_copy(nth(0), target, lon, 1).start()

        make_piece(recv, lon, nth(0), lon)

        @pl.loop(1, chunks)
        def _(i):
            part = nth(i)

            @pl.loop(1, lon_count)
            def _(k):
                target = lax.rem(lon + k, lon_count)
                make_piece(go, target, part, target)
                go_copy(part, target, lon, 0).start()
                go_copy(part, target, lon, 1).start()

            make_piece(recv, lon, part, lon)

    @pl.when(jnp.logical_not(polar))
    def _():
        @pl.loop(0, groups)
        def _(g):
            values = tendency_group(g)
            for c in range(3):
                out_ref[c, pl.ds(aligned(g * SUB), SUB), :] = values[c]

    for copy in table_loads:
        copy.wait()

    cut_start = jnp.where(lat == 0, 0, rows) + lon * share

    @pl.when(polar)
    def _():
        @pl.loop(0, chunks)
        def _(i):
            part = nth(i)
            for k in range(1, lon_count):
                for side in range(2):
                    go_copy(part, lon, lax.rem(lon + k, lon_count), side).wait_recv()
            for d in range(lon_count):
                for t in range(whole):
                    lanes = slice(d * cols + t * LANES, d * cols + (t + 1) * LANES)
                    full[:, lanes] = recv[d, part, slot(t) : slot(t) + 3 * chunk, :]
                if cols % LANES:
                    lanes = slice(d * cols + whole * LANES, (d + 1) * cols)
                    for group in range(3 * per_chunk):
                        at_rows, at_lanes = half_place(group)
                        full[group * SUB : (group + 1) * SUB, lanes] = recv[d, part, at_rows, at_lanes]

            @pl.loop(0, 3 * chunk // SUB)
            def _(g):
                block = pl.ds(aligned(g * SUB), SUB)
                re, im = forward_radix(lambda p: full[block, p * LANES : (p + 1) * LANES], tiles)
                spec[0, block, :LANES] = re[0]
                spec[0, block, LANES:] = re[half]
                for r in range(1, half):
                    spec[r, block, :LANES] = re[r]
                    spec[r, block, LANES:] = im[r]

            wanted = cut_start + part * chunk + lax.broadcasted_iota(jnp.int32, (chunk, 2 * rows), 0)
            hit = wanted == lax.broadcasted_iota(jnp.int32, (chunk, 2 * rows), 1)
            cuts = cut_ref[...].astype(jnp.float32)[None, :]
            limit = jnp.sum(jnp.where(hit, cuts, 0.0), axis=1, keepdims=True)
            limit = jnp.concatenate([limit, limit, limit], axis=0)

            @pl.loop(0, half)
            def _(r):
                z = split_dot(spec[r], fwd, r, False)
                z = jnp.where(bins[r, 0:1, :] <= limit, z * bins[r, 1:2, :], 0.0)
                spec[r] = split_dot(z, fwd, r, True)

            @pl.loop(0, 3 * chunk // SUB)
            def _(g):
                block = pl.ds(aligned(g * SUB), SUB)
                re = [spec[r, block, :LANES] for r in range(half)] + [spec[0, block, LANES:]]
                im = [None] + [spec[r, block, LANES:] for r in range(1, half)]
                x = inverse_radix(re, im, tiles)
                for p in range(tiles):
                    full[block, p * LANES : (p + 1) * LANES] = x[p]

            for d in range(lon_count):
                for t in range(whole):
                    lanes = slice(d * cols + t * LANES, d * cols + (t + 1) * LANES)
                    ret[d, part, slot(t) : slot(t) + 3 * chunk, :] = full[:, lanes]
                if cols % LANES:
                    lanes = slice(d * cols + whole * LANES, (d + 1) * cols)
                    for group in range(3 * per_chunk):
                        at_rows, at_lanes = half_place(group)
                        ret[d, part, at_rows, at_lanes] = full[group * SUB : (group + 1) * SUB, lanes]
            for k in range(1, lon_count):
                back_copy(part, lax.rem(lon + k, lon_count), lon).start()
            unpack(ret, part, lon)

        @pl.loop(0, chunks)
        def _(i):
            part = nth(i)

            @pl.loop(1, lon_count)
            def _(k):
                other = lax.rem(lon + k, lon_count)
                for side in range(2):
                    go_copy(part, other, lon, side).wait_send()
                back_copy(part, lon, other).wait_recv()
                unpack(back, part, other)
                back_copy(part, other, lon).wait_send()


def fused_step(mesh_shape, tables, state_now, state_old, polar_cutoff):
    lat_count, lon_count = mesh_shape
    comps, rows, cols = state_now.shape
    share = rows // lon_count
    total = lon_count * cols
    half = total // LANES // 2
    chunk = chunk_rows(share)
    chunks = share // chunk
    geo, fwd, bins = tables
    groups = comps * chunk // SUB
    piece = (cols // LANES * groups + (groups + 1) // 2 * (cols % LANES > 0)) * SUB
    operands = [
        pltpu.with_memory_space_constraint(jnp.asarray(a), pltpu.HBM)
        for a in (state_now, geo, polar_cutoff, bins, fwd)
    ]
    hbm_spec = pl.BlockSpec(memory_space=pltpu.HBM)
    vmem_spec = pl.BlockSpec(memory_space=pltpu.VMEM)
    dma = pltpu.SemaphoreType.DMA
    filtered = pl.pallas_call(
        functools.partial(step_kernel, lat_count, lon_count, chunk),
        out_shape=jax.ShapeDtypeStruct(state_now.shape, jnp.float32),
        in_specs=[hbm_spec] * 5,
        out_specs=vmem_spec,
        scratch_shapes=[
            pltpu.VMEM((comps, rows + 2 * SUB, cols), jnp.float32),
            pltpu.VMEM((rows, LANES), jnp.float32),
            pltpu.VMEM((2 * rows,), jnp.int32),
            pltpu.VMEM((half, SUB, 2 * LANES), jnp.float32),
            pltpu.VMEM((lon_count, chunks, piece, LANES), jnp.float32),
            pltpu.VMEM((lon_count, chunks, piece, LANES), jnp.float32),
            pltpu.VMEM((lon_count, chunks, piece, LANES), jnp.float32),
            pltpu.VMEM((lon_count, chunks, piece, LANES), jnp.float32),
            pltpu.VMEM((comps * chunk, total), jnp.float32),
            pltpu.VMEM((half, comps * chunk, 2 * LANES), jnp.float32),
            pltpu.VMEM((2, half, 2 * LANES, 2 * LANES), jnp.bfloat16),
            pltpu.VMEM((2, comps, SUB, LANES), jnp.float32),
            pltpu.VMEM((2, comps, SUB, LANES), jnp.float32),
            dma, dma((4,)), dma((2,)), dma((2,)), dma((2,)), dma((2,)),
            dma((2, lon_count, chunks)), dma((2, lon_count, chunks)),
            dma((lon_count, chunks)), dma((lon_count, chunks)),
        ],
        compiler_params=pltpu.CompilerParams(
            collective_id=0, has_side_effects=True, vmem_limit_bytes=48 * 1024 * 1024
        ),
    )(*operands)
    return state_old + step_scale * filtered


def chunk_rows(share):
    for parts in (3, 4, 5):
        if share % (parts * SUB) == 0:
            return share // parts
    return 0


def solution(mesh):
    lat_count, lon_count = mesh.shape["lat"], mesh.shape["lon"]

    def step(state_now, state_old, polar_cutoff):
        comps, lat_total, lon_total = state_now.shape
        rows, cols = lat_total // lat_count, lon_total // lon_count
        share = rows // lon_count
        fits = (
            lat_count >= 4 and lat_total == 4 * rows and rows % lon_count == 0
            and chunk_rows(share) > 0 and cols % (LANES // 2) == 0 and cols >= 2 * LANES and rows // SUB <= LANES
            and lon_total % (2 * LANES) == 0 and comps == 3 * mesh.shape["ens"]
        )
        body = per_device
        if fits:
            tables = (geometry_table(lat_total, lon_total), *spectral_tables(lon_total))
            body = functools.partial(fused_step, (lat_count, lon_count), tables)
        return jax.shard_map(
            body,
            mesh=mesh,
            in_specs=(P("ens", "lat", "lon"), P("ens", "lat", "lon"), P()),
            out_specs=P("ens", "lat", "lon"),
            check_vma=False,
        )(state_now, state_old, polar_cutoff)

    return step
```

```python
import functools
import math

import jax
import jax.numpy as jnp
import numpy as np
from jax import lax
from jax.experimental import pallas as pl
from jax.experimental.pallas import tpu as pltpu
from jax.sharding import PartitionSpec as P

LANES = 128
SUB = 8
MESH = pl.DeviceIdType.MESH
step_scale = 0.2
coriolis = 2.0
gravity = 1.0
highest = lax.Precision.HIGHEST


def padded(value, sides, width, wrap):
    for axis, dim in sides:
        devices, length = (lax.axis_size(axis), value.shape[dim])
        up = [(i, (i + 1) % devices) for i in range(devices if wrap else devices - 1)]
        down = [(j, i) for i, j in up]
        last = lax.slice_in_dim(value, length - width, length, axis=dim)
        leading = lax.slice_in_dim(value, 0, width, axis=dim)
        before = lax.ppermute(last, axis, up)
        after = lax.ppermute(leading, axis, down)
        value = jnp.concatenate([before, value, after], axis=dim)
    return value


def latitude_terms(row_index, lat_total):
    distance = jnp.minimum(row_index + 0.5, lat_total - row_index - 0.5)
    cosine_lat = jnp.sin(math.pi * distance / lat_total)
    sine_lat = -jnp.cos(math.pi * (row_index + 0.5) / lat_total)
    return (cosine_lat, sine_lat)


def tendencies(lat_padded, lon_padded, cos_ext, sine_lat, lat_total, lon_total):
    cosine_lat = cos_ext[1:-1]
    zonal_scale = (lon_total / (4.0 * lat_total) / cosine_lat)[:, None]
    metric = math.pi / lat_total * sine_lat / cosine_lat
    depth_lon, east_lon, north_lon = (lon_padded[0], lon_padded[1], lon_padded[2])
    depth_lat, east_lat, north_lat = (lat_padded[0], lat_padded[1], lat_padded[2])
    east = east_lon[:, 1:-1]
    north = north_lon[:, 1:-1]

    def zonal_change(field):
        return zonal_scale * (field[:, 2:] - field[:, :-2])

    def northward_change(field):
        return 0.5 * (field[2:] - field[:-2])

    mass_flux = depth_lat * north_lat * cos_ext[:, None]
    tend_depth = (
        -zonal_change(depth_lon * east_lon) - northward_change(mass_flux) / cosine_lat[:, None]
    )
    turning = coriolis * sine_lat[:, None] + metric[:, None] * east
    tend_east = (
        -east * zonal_change(east_lon)
        - north * northward_change(east_lat)
        + turning * north
        - gravity * zonal_change(depth_lon)
    )
    tend_north = (
        -east * zonal_change(north_lon)
        - north * northward_change(north_lat)
        - turning * east
        - gravity * northward_change(depth_lat)
    )
    return jnp.stack([tend_depth, tend_east, tend_north])


def angle_table(first_count, second_count, period):
    first_idx = jnp.arange(first_count, dtype=jnp.int32)
    second_idx = jnp.arange(second_count, dtype=jnp.int32)
    turns = first_idx[:, None] * second_idx[None, :] % period
    phase = turns.astype(jnp.float32) * (2.0 * math.pi / period)
    return (jnp.cos(phase), jnp.sin(phase))


def low_pass(signal, cutoff):
    count, length = signal.shape
    first = 1
    probe = 1
    while probe * probe <= length:
        if length % probe == 0:
            first = probe
        probe = probe + 1
    second = length // first
    cos_first, sin_first = angle_table(first, first, first)
    cos_second, sin_second = angle_table(second, second, second)
    cos_twist, sin_twist = angle_table(first, second, length)
    grid = signal.reshape(count, first, second)
    part_re = jnp.einsum("cpq,pk->ckq", grid, cos_first, precision=highest)
    part_im = -jnp.einsum("cpq,pk->ckq", grid, sin_first, precision=highest)
    twist_re = part_re * cos_twist + part_im * sin_twist
    twist_im = part_im * cos_twist - part_re * sin_twist
    spec_re = jnp.einsum("ckq,qm->ckm", twist_re, cos_second, precision=highest) + jnp.einsum(
        "ckq,qm->ckm", twist_im, sin_second, precision=highest
    )
    spec_im = jnp.einsum("ckq,qm->ckm", twist_im, cos_second, precision=highest) - jnp.einsum(
        "ckq,qm->ckm", twist_re, sin_second, precision=highest
    )
    wave = (
        jnp.arange(first, dtype=jnp.int32)[:, None]
        + first * jnp.arange(second, dtype=jnp.int32)[None, :]
    )
    limit = cutoff[:, None, None]
    keep = ((wave[None] <= limit) | (wave[None] >= length - limit)).astype(jnp.float32) * (
        1.0 / length
    )
    spec_re = spec_re * keep
    spec_im = spec_im * keep
    back_re = jnp.einsum("ckm,mq->ckq", spec_re, cos_second, precision=highest) - jnp.einsum(
        "ckm,mq->ckq", spec_im, sin_second, precision=highest
    )
    back_im = jnp.einsum("ckm,mq->ckq", spec_im, cos_second, precision=highest) + jnp.einsum(
        "ckm,mq->ckq", spec_re, sin_second, precision=highest
    )
    turn_re = back_re * cos_twist - back_im * sin_twist
    turn_im = back_im * cos_twist + back_re * sin_twist
    result = jnp.einsum("ckq,kp->cpq", turn_re, cos_first, precision=highest) - jnp.einsum(
        "ckq,kp->cpq", turn_im, sin_first, precision=highest
    )
    return result.reshape(count, length)


def per_device(state_now, state_old, polar_cutoff):
    lat_rows = state_now.shape[1]
    lon_cols = state_now.shape[2]
    lat_count = lax.axis_size("lat")
    lon_count = lax.axis_size("lon")
    lat_total = lat_rows * lat_count
    lon_total = lon_cols * lon_count
    lat_place = lax.axis_index("lat")
    lat_padded = padded(state_now, (("lat", 1),), 1, False)
    lon_padded = padded(state_now, (("lon", 2),), 1, True)
    row_index = (lat_place * lat_rows + jnp.arange(-1, lat_rows + 1, dtype=jnp.int32)).astype(
        jnp.float32
    )
    cos_ext, sin_ext = latitude_terms(row_index, lat_total)
    forcing = tendencies(lat_padded, lon_padded, cos_ext, sin_ext[1:-1], lat_total, lon_total)
    groups = lat_count * lon_count
    share = lat_rows // groups
    member = lax.axis_index(("lat", "lon"))
    south_cut = lax.dynamic_slice_in_dim(polar_cutoff, member * share, share)
    north_cut = lax.dynamic_slice_in_dim(polar_cutoff, lat_rows + member * share, share)
    band_cut = jnp.concatenate([south_cut, north_cut])
    block = lax.all_to_all(forcing, ("lat", "lon"), split_axis=1, concat_axis=2, tiled=True)
    items = block.shape[0]
    wide = block.shape[2]
    south_rows = block[:, :, :lon_total]
    north_rows = block[:, :, wide - lon_total :]
    polar_rows = jnp.concatenate([south_rows, north_rows], axis=1)
    smooth = low_pass(polar_rows.reshape(items * 2 * share, lon_total), jnp.tile(band_cut, items))
    smooth = smooth.reshape(items, 2 * share, lon_total)
    rebuilt = jnp.concatenate(
        [smooth[:, :share], block[:, :, lon_total : wide - lon_total], smooth[:, share:]], axis=2
    )
    filtered = lax.all_to_all(rebuilt, ("lat", "lon"), split_axis=2, concat_axis=1, tiled=True)
    return state_old + step_scale * filtered


def spectral_tables(total):
    tiles = total // LANES
    half = tiles // 2
    q = np.arange(LANES)[:, None]
    m = np.arange(LANES)[None, :]
    forward = np.zeros((half, 2 * LANES, 2 * LANES))
    wave = np.zeros((half, 2 * LANES), np.int64)

    def angle(k):
        return 2.0 * np.pi * ((q * k) % total) / total

    mid = LANES // 2
    re_m = np.arange(mid + 1)[None, :]
    im_m = np.arange(1, mid)[None, :]
    k_re, k_im = tiles * re_m, tiles * im_m
    forward[0, :LANES, : mid + 1] = np.cos(angle(k_re))
    forward[0, :LANES, mid + 1 : LANES] = -np.sin(angle(k_im))
    k_odd = half + tiles * np.arange(mid)[None, :]
    odd = np.concatenate([np.cos(angle(k_odd)), -np.sin(angle(k_odd))], axis=1)
    forward[0, LANES:, LANES:] = odd
    wave[0] = np.concatenate([k_re[0], k_im[0], k_odd[0], k_odd[0]])
    for r in range(1, half):
        k = r + tiles * m
        c, s = np.cos(angle(k)), np.sin(angle(k))
        forward[r] = np.block([[c, -s], [s, c]])
        wave[r] = np.concatenate([k[0], k[0]])
    wave = np.minimum(wave, total - wave)

    def split(a):
        a = a.astype(np.float32)
        hi = a.astype(jnp.bfloat16)
        lo = (a - hi.astype(np.float32)).astype(jnp.bfloat16)
        return np.stack([hi, lo])

    bins = np.zeros((half, SUB, 2 * LANES), np.float32)
    bins[:, 0] = wave
    bins[:, 1] = 2.0 / total
    bins[0, 1, [0, mid]] = 1.0 / total
    return split(forward), bins


def geometry_table(lat_total, lon_total):
    j = np.arange(lat_total, dtype=np.float64)

    def cosine(row):
        return np.sin(np.pi * np.minimum(row + 0.5, lat_total - row - 0.5) / lat_total)

    c = cosine(j)
    s = -np.cos(np.pi * (j + 0.5) / lat_total)
    table = np.zeros((lat_total, LANES))
    table[:, 0] = lon_total / (4.0 * lat_total * c)
    table[:, 1] = 0.5 * cosine(j + 1) / c
    table[:, 2] = 0.5 * cosine(j - 1) / c
    table[:, 3] = coriolis * s
    table[:, 4] = np.pi / lat_total * s / c
    return table.astype(np.float32)


def forward_radix(tile, tiles):
    half = tiles // 2
    x = [tile(p) for p in range(tiles)]
    even = [None] * (half + 1)
    odd = [None] * (half + 1)
    even[0], even[half] = x[0], x[half]
    for p in range(1, half):
        even[p] = x[p] + x[tiles - p]
        odd[p] = x[p] - x[tiles - p]
    re, im = [None] * (half + 1), [None] * (half + 1)
    for r in range(half // 2 + 1):
        e = parity_sum([(even[p], math.cos(2 * math.pi * p * r / tiles)) for p in range(0, half + 1, 2)])
        o = parity_sum([(even[p], math.cos(2 * math.pi * p * r / tiles)) for p in range(1, half + 1, 2)])
        re[r] = e + o
        re[half - r] = e - o
        if 0 < r:
            es = parity_sum([(odd[p], math.sin(2 * math.pi * p * r / tiles)) for p in range(2, half, 2)])
            os = parity_sum([(odd[p], math.sin(2 * math.pi * p * r / tiles)) for p in range(1, half, 2)])
            im[r] = -(es + os)
            im[half - r] = es - os
    return re, im


def parity_sum(terms):
    total = None
    for value, factor in terms:
        if abs(factor - 1.0) < 1e-12:
            term = value
        elif abs(factor + 1.0) < 1e-12:
            term = -value
        elif abs(factor) < 1e-12:
            continue
        else:
            term = value * np.float32(factor)
        total = term if total is None else total + term
    return total if total is not None else jnp.zeros_like(terms[0][0])


def inverse_radix(re, im, tiles):
    half = tiles // 2
    x = [None] * tiles
    for p in range(half // 2 + 1):
        ce = parity_sum([(re[r], math.cos(2 * math.pi * p * r / tiles)) for r in range(0, half + 1, 2)])
        co = parity_sum([(re[r], math.cos(2 * math.pi * p * r / tiles)) for r in range(1, half + 1, 2)])
        if p == 0:
            x[0] = ce + co
            x[half] = ce - co
            continue
        se = parity_sum([(im[r], math.sin(2 * math.pi * p * r / tiles)) for r in range(2, half, 2)])
        so = parity_sum([(im[r], math.sin(2 * math.pi * p * r / tiles)) for r in range(1, half, 2)])
        c, s = ce + co, se + so
        x[p] = c - s
        x[tiles - p] = c + s
        c, s = ce - co, so - se
        x[half - p] = c - s
        x[half + p] = c + s
    return x


def split_dot(value, table, r, transpose):
    hi = value.astype(jnp.bfloat16)
    lo = (value - hi.astype(jnp.float32)).astype(jnp.bfloat16)
    big, small = table[0, r], table[1, r]
    dims = (((1,), (1 if transpose else 0,)), ((), ()))

    def dot(a, b):
        return lax.dot_general(a, b, dims, preferred_element_type=jnp.float32)

    return dot(hi, big) + dot(lo, big) + dot(hi, small)


def step_kernel(
    lat_count, lon_count, chunk,
    x_hbm, old_hbm, geo_hbm, cut_hbm, bins_hbm, fwd_hbm, out_ref,
    old, xp, geo, cut_ref, bins, go, recv, ret, back, full, spec, fwd, col_send, col_recv,
    load_sem, table_sem, row_send_sem, row_recv_sem, col_send_sem, col_recv_sem,
    go_send, go_recv, back_send, back_recv,
):
    rows, cols = out_ref.shape[1], out_ref.shape[2]
    share = rows // lon_count
    chunks = share // chunk
    groups = rows // SUB
    tiles = lon_count * cols // LANES
    half = tiles // 2
    lat = lax.axis_index("lat")
    lon = lax.axis_index("lon")
    west = lax.rem(lon + lon_count - 1, lon_count)
    east = lax.rem(lon + 1, lon_count)
    polar = jnp.logical_or(lat == 0, lat == lat_count - 1)
    has_south = lat > 0
    has_north = lat < lat_count - 1

    load = pltpu.make_async_copy(x_hbm, xp.at[:, pl.ds(SUB, rows), :], load_sem)
    load.start()
    geo_load = pltpu.make_async_copy(
        geo_hbm.at[pl.ds(pl.multiple_of(lat * rows, SUB), rows), :], geo, table_sem.at[0]
    )
    geo_load.start()
    table_loads = [
        pltpu.make_async_copy(src, dst, table_sem.at[i + 1])
        for i, (src, dst) in enumerate([(fwd_hbm, fwd), (bins_hbm, bins), (cut_hbm, cut_ref), (old_hbm, old)])
    ]
    for copy in table_loads:
        copy.start()

    barrier = pltpu.get_barrier_semaphore()
    for k in range(1, lon_count):
        pl.semaphore_signal(
            barrier, inc=1, device_id={"lon": lax.rem(lon + k, lon_count)}, device_id_type=MESH
        )

    @pl.when(has_south)
    def _():
        pl.semaphore_signal(barrier, inc=1, device_id={"lat": lat - 1}, device_id_type=MESH)

    @pl.when(has_north)
    def _():
        pl.semaphore_signal(barrier, inc=1, device_id={"lat": lat + 1}, device_id_type=MESH)

    load.wait()
    lane = lax.broadcasted_iota(jnp.int32, (SUB, LANES), 1)

    packed = [jnp.zeros((SUB, LANES), jnp.float32) for _ in range(6)]
    for g in range(groups):
        here = lane == g
        for c in range(3):
            block = slice(SUB + g * SUB, 2 * SUB + g * SUB)
            packed[2 * c] = jnp.where(here, xp[c, block, 0:1], packed[2 * c])
            packed[2 * c + 1] = jnp.where(here, xp[c, block, cols - 1 : cols], packed[2 * c + 1])
    for c in range(3):
        col_send[0, c] = packed[2 * c]
        col_send[1, c] = packed[2 * c + 1]

    pl.semaphore_wait(
        barrier, lon_count - 1 + has_south.astype(jnp.int32) + has_north.astype(jnp.int32)
    )

    def to_south():
        return pltpu.make_async_remote_copy(
            src_ref=x_hbm.at[:, pl.ds(0, SUB), :], dst_ref=xp.at[:, pl.ds(rows + SUB, SUB), :],
            send_sem=row_send_sem.at[0], recv_sem=row_recv_sem.at[0],
            device_id={"lat": lat - 1}, device_id_type=MESH,
        )

    def to_north():
        return pltpu.make_async_remote_copy(
            src_ref=x_hbm.at[:, pl.ds(rows - SUB, SUB), :], dst_ref=xp.at[:, pl.ds(0, SUB), :],
            send_sem=row_send_sem.at[1], recv_sem=row_recv_sem.at[1],
            device_id={"lat": lat + 1}, device_id_type=MESH,
        )

    @pl.when(has_south)
    def _():
        to_south().start()

    @pl.when(has_north)
    def _():
        to_north().start()

    zero_rows = jnp.zeros((3, SUB, cols), jnp.float32)

    @pl.when(jnp.logical_not(has_south))
    def _():
        xp[:, 0:SUB, :] = zero_rows

    @pl.when(jnp.logical_not(has_north))
    def _():
        xp[:, rows + SUB : rows + 2 * SUB, :] = zero_rows

    def column_copy(side, target):
        return pltpu.make_async_remote_copy(
            src_ref=col_send.at[side], dst_ref=col_recv.at[side],
            send_sem=col_send_sem.at[side], recv_sem=col_recv_sem.at[side],
            device_id={"lon": target}, device_id_type=MESH,
        )

    first_out = column_copy(0, west)
    last_out = column_copy(1, east)
    first_out.start()
    last_out.start()
    geo_load.wait()
    sub_idx = lax.broadcasted_iota(jnp.int32, (SUB, cols), 0)

    def tendency_group(g, edges=True):
        start = pl.multiple_of(g * SUB, SUB)
        terms = geo[pl.ds(start, SUB), :]
        zonal, up, down, turn, metric = [terms[:, i : i + 1] for i in range(5)]
        cur, north, south, diff, east_of, west_of = [], [], [], [], [], []
        for c in range(3):
            before = xp[c, pl.ds(start, SUB), :]
            here = xp[c, pl.ds(pl.multiple_of(start + SUB, SUB), SUB), :]
            after = xp[c, pl.ds(pl.multiple_of(start + 2 * SUB, SUB), SUB), :]
            north.append(pltpu.roll(jnp.where(sub_idx == 0, after, here), SUB - 1, 0))
            south.append(pltpu.roll(jnp.where(sub_idx == SUB - 1, before, here), 1, 0))
            if edges:
                on = lane == g
                right = jnp.sum(jnp.where(on, col_recv[0, c], 0.0), axis=1, keepdims=True)
                left = jnp.sum(jnp.where(on, col_recv[1, c], 0.0), axis=1, keepdims=True)
            else:
                right, left = here[:, -1:], here[:, :1]
            east_of.append(jnp.concatenate([here[:, 1:], right], axis=1))
            west_of.append(jnp.concatenate([left, here[:, :-1]], axis=1))
            cur.append(here)
        h, u, v = cur
        t_h = -zonal * (east_of[0] * east_of[1] - west_of[0] * west_of[1]) - (
            up * (north[0] * north[2]) - down * (south[0] * south[2])
        )
        turning = turn + metric * u
        zu = zonal * u
        hv = 0.5 * v
        t_u = (
            turning * v - zu * (east_of[1] - west_of[1]) - hv * (north[1] - south[1])
            - zonal * (east_of[0] - west_of[0])
        )
        t_v = (
            -turning * u - zu * (east_of[2] - west_of[2]) - hv * (north[2] - south[2])
            - 0.5 * (north[0] - south[0])
        )
        return t_h, t_u, t_v

    def halos_arrive():
        first_out.wait()
        last_out.wait()

        @pl.when(has_south)
        def _():
            to_south().wait_send()
            to_north().wait_recv()

        @pl.when(has_north)
        def _():
            to_north().wait_send()
            to_south().wait_recv()

    near = (lon_count + 1) // 2
    side_start = lon // near * near

    def partner(k):
        if lon_count % 2:
            return lax.rem(lon + k, lon_count)
        place = lon - side_start
        across = near - side_start + lax.rem(place + k - 1, near)
        beside = side_start + lax.rem(place + k - near, near)
        return jnp.where(k <= near, across, beside)

    def aligned(i):
        return pl.multiple_of(i, SUB)

    per_chunk = chunk // SUB
    whole = cols // LANES
    half_at = whole * 3 * chunk

    def half_place(group):
        return pl.ds(half_at + group // 2 * SUB, SUB), pl.ds(group % 2 * (LANES // 2), LANES // 2)

    inner = (whole - 1) * 3 * chunk
    piece = go.shape[2]

    def slot(tile):
        return ((tile + whole - 1) % whole) * 3 * chunk

    def go_copy(part, target, source, side):
        span = pl.ds(0, inner) if side == 0 else pl.ds(inner, piece - inner)
        return pltpu.make_async_remote_copy(
            src_ref=go.at[target, part, span, :], dst_ref=recv.at[source, part, span, :],
            send_sem=go_send.at[side, target, part], recv_sem=go_recv.at[side, source, part],
            device_id={"lon": target}, device_id_type=MESH,
        )

    def back_copy(part, target, source):
        return pltpu.make_async_remote_copy(
            src_ref=ret.at[target, part], dst_ref=back.at[source, part],
            send_sem=back_send.at[target, part], recv_sem=back_recv.at[source, part],
            device_id={"lon": target}, device_id_type=MESH,
        )

    def make_piece(buf, place, part, target, inside=True, outside=True):
        first = (target * share + part * chunk) // SUB
        for i in range(per_chunk):
            values = tendency_group(first + i, edges=outside)
            for c in range(3):
                group = c * per_chunk + i
                for t in range(whole):
                    if outside if t == 0 else inside:
                        buf[place, part, slot(t) + group * SUB : slot(t) + (group + 1) * SUB, :] = (
                            values[c][:, t * LANES : (t + 1) * LANES]
                        )
                if outside and cols % LANES:
                    at_rows, at_lanes = half_place(group)
                    buf[place, part, at_rows, at_lanes] = values[c][:, whole * LANES :]

    def unpack(buf, part, source):
        first = source * share + part * chunk
        for c in range(3):
            for t in range(whole):
                at = (c, pl.ds(aligned(first), chunk), slice(t * LANES, (t + 1) * LANES))
                value = buf[source, part, pl.ds(slot(t) + c * chunk, chunk), :]
                out_ref[at] = old[at] + step_scale * value
            if cols % LANES:
                for i in range(per_chunk):
                    at_rows, at_lanes = half_place(c * per_chunk + i)
                    at = (c, pl.ds(aligned(first + i * SUB), SUB), slice(whole * LANES, cols))
                    out_ref[at] = old[at] + step_scale * buf[source, part, at_rows, at_lanes]

    def nth(i):
        return lax.rem(i + 1, chunks)

    @pl.when(polar)
    def _():
        @pl.loop(1, lon_count)
        def _(k):
            target = partner(k)
            make_piece(go, target, nth(0), target, outside=False)
            go_copy(nth(0), target, lon, 0).start()

    halos_arrive()

    @pl.when(polar)
    def _():
        @pl.loop(1, lon_count)
        def _(k):
            target = partner(k)
            make_piece(go, target, nth(0), target, inside=False)
            go_copy(nth(0), target, lon, 1).start()

        make_piece(recv, lon, nth(0), lon)

        @pl.loop(1, chunks)
        def _(i):
            part = nth(i)

            @pl.loop(1, lon_count)
            def _(k):
                target = partner(k)
                make_piece(go, target, part, target)
                go_copy(part, target, lon, 0).start()
                go_copy(part, target, lon, 1).start()

            make_piece(recv, lon, part, lon)

    for copy in table_loads:
        copy.wait()

    @pl.when(jnp.logical_not(polar))
    def _():
        @pl.loop(0, groups)
        def _(g):
            values = tendency_group(g)
            for c in range(3):
                at = (c, pl.ds(aligned(g * SUB), SUB), slice(None))
                out_ref[at] = old[at] + step_scale * values[c]

    cut_start = jnp.where(lat == 0, 0, rows) + lon * share

    @pl.when(polar)
    def _():
        @pl.loop(0, chunks)
        def _(i):
            part = nth(i)
            for k in range(1, lon_count):
                for side in range(2):
                    go_copy(part, lon, partner(k), side).wait_recv()
            for d in range(lon_count):
                for t in range(whole):
                    lanes = slice(d * cols + t * LANES, d * cols + (t + 1) * LANES)
                    full[:, lanes] = recv[d, part, slot(t) : slot(t) + 3 * chunk, :]
                if cols % LANES:
                    lanes = slice(d * cols + whole * LANES, (d + 1) * cols)
                    for group in range(3 * per_chunk):
                        at_rows, at_lanes = half_place(group)
                        full[group * SUB : (group + 1) * SUB, lanes] = recv[d, part, at_rows, at_lanes]

            @pl.loop(0, 3 * chunk // SUB)
            def _(g):
                block = pl.ds(aligned(g * SUB), SUB)
                re, im = forward_radix(lambda p: full[block, p * LANES : (p + 1) * LANES], tiles)
                spec[0, block, :LANES] = re[0]
                spec[0, block, LANES:] = re[half]
                for r in range(1, half):
                    spec[r, block, :LANES] = re[r]
                    spec[r, block, LANES:] = im[r]

            wanted = cut_start + part * chunk + lax.broadcasted_iota(jnp.int32, (chunk, 2 * rows), 0)
            hit = wanted == lax.broadcasted_iota(jnp.int32, (chunk, 2 * rows), 1)
            cuts = cut_ref[...].astype(jnp.float32)[None, :]
            limit = jnp.sum(jnp.where(hit, cuts, 0.0), axis=1, keepdims=True)
            limit = jnp.concatenate([limit, limit, limit], axis=0)

            @pl.loop(0, half)
            def _(r):
                z = split_dot(spec[r], fwd, r, False)
                z = jnp.where(bins[r, 0:1, :] <= limit, z * bins[r, 1:2, :], 0.0)
                spec[r] = split_dot(z, fwd, r, True)

            @pl.loop(0, 3 * chunk // SUB)
            def _(g):
                block = pl.ds(aligned(g * SUB), SUB)
                re = [spec[r, block, :LANES] for r in range(half)] + [spec[0, block, LANES:]]
                im = [None] + [spec[r, block, LANES:] for r in range(1, half)]
                x = inverse_radix(re, im, tiles)
                for p in range(tiles):
                    full[block, p * LANES : (p + 1) * LANES] = x[p]

            for d in range(lon_count):
                for t in range(whole):
                    lanes = slice(d * cols + t * LANES, d * cols + (t + 1) * LANES)
                    ret[d, part, slot(t) : slot(t) + 3 * chunk, :] = full[:, lanes]
                if cols % LANES:
                    lanes = slice(d * cols + whole * LANES, (d + 1) * cols)
                    for group in range(3 * per_chunk):
                        at_rows, at_lanes = half_place(group)
                        ret[d, part, at_rows, at_lanes] = full[group * SUB : (group + 1) * SUB, lanes]
            for k in range(1, lon_count):
                back_copy(part, partner(k), lon).start()
            unpack(ret, part, lon)

        @pl.loop(0, chunks)
        def _(i):
            part = nth(i)

            @pl.loop(1, lon_count)
            def _(k):
                other = partner(k)
                for side in range(2):
                    go_copy(part, other, lon, side).wait_send()
                back_copy(part, lon, other).wait_recv()
                unpack(back, part, other)
                back_copy(part, other, lon).wait_send()


def fused_step(mesh_shape, tables, state_now, state_old, polar_cutoff):
    lat_count, lon_count = mesh_shape
    comps, rows, cols = state_now.shape
    share = rows // lon_count
    total = lon_count * cols
    half = total // LANES // 2
    chunk = chunk_rows(share)
    chunks = share // chunk
    geo, fwd, bins = tables
    groups = comps * chunk // SUB
    piece = (cols // LANES * groups + (groups + 1) // 2 * (cols % LANES > 0)) * SUB
    operands = [
        pltpu.with_memory_space_constraint(jnp.asarray(a), pltpu.HBM)
        for a in (state_now, state_old, geo, polar_cutoff, bins, fwd)
    ]
    hbm_spec = pl.BlockSpec(memory_space=pltpu.HBM)
    vmem_spec = pl.BlockSpec(memory_space=pltpu.VMEM)
    dma = pltpu.SemaphoreType.DMA
    filtered = pl.pallas_call(
        functools.partial(step_kernel, lat_count, lon_count, chunk),
        out_shape=jax.ShapeDtypeStruct(state_now.shape, jnp.float32),
        in_specs=[hbm_spec] * 6,
        out_specs=vmem_spec,
        scratch_shapes=[
            pltpu.VMEM((comps, rows, cols), jnp.float32),
            pltpu.VMEM((comps, rows + 2 * SUB, cols), jnp.float32),
            pltpu.VMEM((rows, LANES), jnp.float32),
            pltpu.VMEM((2 * rows,), jnp.int32),
            pltpu.VMEM((half, SUB, 2 * LANES), jnp.float32),
            pltpu.VMEM((lon_count, chunks, piece, LANES), jnp.float32),
            pltpu.VMEM((lon_count, chunks, piece, LANES), jnp.float32),
            pltpu.VMEM((lon_count, chunks, piece, LANES), jnp.float32),
            pltpu.VMEM((lon_count, chunks, piece, LANES), jnp.float32),
            pltpu.VMEM((comps * chunk, total), jnp.float32),
            pltpu.VMEM((half, comps * chunk, 2 * LANES), jnp.float32),
            pltpu.VMEM((2, half, 2 * LANES, 2 * LANES), jnp.bfloat16),
            pltpu.VMEM((2, comps, SUB, LANES), jnp.float32),
            pltpu.VMEM((2, comps, SUB, LANES), jnp.float32),
            dma, dma((5,)), dma((2,)), dma((2,)), dma((2,)), dma((2,)),
            dma((2, lon_count, chunks)), dma((2, lon_count, chunks)),
            dma((lon_count, chunks)), dma((lon_count, chunks)),
        ],
        compiler_params=pltpu.CompilerParams(
            collective_id=0, has_side_effects=True, vmem_limit_bytes=48 * 1024 * 1024
        ),
    )(*operands)
    return filtered


def chunk_rows(share):
    for parts in (3, 4, 5):
        if share % (parts * SUB) == 0:
            return share // parts
    return 0


def solution(mesh):
    lat_count, lon_count = mesh.shape["lat"], mesh.shape["lon"]

    def step(state_now, state_old, polar_cutoff):
        comps, lat_total, lon_total = state_now.shape
        rows, cols = lat_total // lat_count, lon_total // lon_count
        share = rows // lon_count
        fits = (
            lat_count >= 4 and lat_total == 4 * rows and rows % lon_count == 0
            and chunk_rows(share) > 0 and cols % (LANES // 2) == 0 and cols >= 2 * LANES and rows // SUB <= LANES
            and lon_total % (2 * LANES) == 0 and comps == 3 * mesh.shape["ens"]
        )
        body = per_device
        if fits:
            tables = (geometry_table(lat_total, lon_total), *spectral_tables(lon_total))
            body = functools.partial(fused_step, (lat_count, lon_count), tables)
        return jax.shard_map(
            body,
            mesh=mesh,
            in_specs=(P("ens", "lat", "lon"), P("ens", "lat", "lon"), P()),
            out_specs=P("ens", "lat", "lon"),
            check_vma=False,
        )(state_now, state_old, polar_cutoff)

    return step
```
